512 devices in a mesh: seq: 128 (over y, z, core), head: 4 (over x).
Axes of the slice: x: 4, y: 8, z: 8, core: 2. Of those that a mesh axis runs over, the one named last changes fastest.
Arguments:
- queries: bfloat16 [65536, 2048], P('seq', 'head'), may hold values from -4 to 4
- keys: bfloat16 [65536, 2048], P('seq', 'head'), may hold values from -4 to 4
- values: bfloat16 [65536, 2048], P('seq', 'head'), may hold values from -6 to 6
- rates: float32 [65536, 4], P('seq', 'head'), may hold values from 0.02 to 0.3
- fast: bfloat16 [4, 3, 512, 512], P('head'), may hold values from -0.25 to 0.25
- momentum: float32 [4, 3, 512, 512], P('head', None, 'seq'), may hold values from -0.24 to 0.24
- out_proj: bfloat16 [2048, 2048], P('seq', 'head'), may hold values from -0.125 to 0.125
Outputs:
- mixed: bfloat16 [65536, 2048], P('seq', 'head')
- new_momentum: float32 [4, 3, 512, 512], P('head', None, 'seq')
The draws below stay inside these ranges and needn't reach their ends.
All inputs are finite; a program needn't handle non-finite values.
Results may differ from the reference program's by a relative error of at most 0.0094.
Values may be sent and summed in bfloat16 or wider, within the bound.
A program may use at most 64 MiB of HBM per device.

```python
import math
import jax
import jax.numpy as jnp
from jax import lax

HD = 512
HEADS = 4
D = 2048
WINDOW = 512
TOKENS = 65536


def draw_queries(key, part):
    drawn = jnp.clip(jax.random.normal(jax.random.fold_in(key, 11), (TOKENS, D), jnp.float32), -4.0, 4.0)
    return drawn.astype(jnp.bfloat16)


def draw_keys(key, part):
    drawn = jnp.clip(jax.random.normal(jax.random.fold_in(key, 12), (TOKENS, D), jnp.float32), -4.0, 4.0)
    return drawn.astype(jnp.bfloat16)


def block_levels(own_key, shape, cuts, smallest, top_value):
    level = 1.0
    for position, blocks in cuts:
        heights = jax.random.uniform(jax.random.fold_in(jax.random.fold_in(own_key, 6), position), (blocks,), jnp.float32, smallest / len(cuts), top_value / len(cuts))
        level = level * jnp.repeat(jnp.exp(heights), shape[position] // blocks).reshape((-1,) + (1,) * (len(shape) - 1 - position))
    return level


def normal_values(key, extent, spread, bound, split=(), dtype=jnp.bfloat16):
    array = spread * jax.random.normal(key, extent, jnp.float32)
    if split:
        array = array * block_levels(key, extent, split, -0.22, 0.18)
    return jnp.clip(array, -bound, bound).astype(dtype)


def setup_inputs(seed: int = 0) -> dict:
    arg_keys = jax.random.split(jax.random.key(seed), 8)
    queries = draw_queries(jax.random.fold_in(arg_keys[7], 71), 0)
    keys = draw_keys(jax.random.fold_in(arg_keys[7], 71), 0)
    values = normal_values(arg_keys[2], (TOKENS, D), 1.0, 6.0, ((0, 128), (1, 4)))
    rates = jnp.clip(jnp.exp(math.log(0.3) - 2.7080503 * jax.random.uniform(arg_keys[3], (TOKENS, HEADS), jnp.float32) ** block_levels(arg_keys[3], (TOKENS, HEADS), ((0, 128), (1, 4)), -0.2, 0.2)), 0.02, 0.3)
    fast = normal_values(arg_keys[4], (HEADS, 3, HD, HD), HD ** -0.5, 0.25, ((0, 4),))
    momentum = normal_values(arg_keys[5], (HEADS, 3, HD, HD), 0.04, 0.24, ((0, 4), (2, 128)), jnp.float32)
    out_proj = normal_values(arg_keys[6], (D, D), D ** -0.5, 0.125, ((0, 128), (1, 4)))
    return dict(queries=queries, keys=keys, values=values, rates=rates, fast=fast, momentum=momentum, out_proj=out_proj)


MOMENTUM_DECAY = 0.9
NORM_EPS = 1e-06
NEG_LARGE = -1e+30

def times_transposed(left, right):
    return lax.dot_general(left, right, (((1,), (1,)), ((), ())), preferred_element_type=jnp.float32)

def contract_rows(left, right):
    return lax.dot_general(left, right, (((0,), (0,)), ((), ())), preferred_element_type=jnp.float32)

def fast_gradients(keys_head, values_head, rates_head, weights, grad_scale):
    h_gate = times_transposed(keys_head, weights[0])
    h_up = times_transposed(keys_head, weights[1])
    sigma = jax.nn.sigmoid(h_gate)
    gated = (h_gate * sigma * h_up).astype(jnp.bfloat16)
    errors = (-grad_scale * rates_head * values_head.astype(jnp.float32)).astype(jnp.bfloat16)
    grad_down = contract_rows(errors, gated)
    back = jnp.dot(errors, weights[2], preferred_element_type=jnp.float32)
    d_gate = (back * h_up * sigma * (1.0 + h_gate * (1.0 - sigma))).astype(jnp.bfloat16)
    d_up = (back * h_gate * sigma).astype(jnp.bfloat16)
    grad_gate = contract_rows(d_gate, keys_head)
    grad_up = contract_rows(d_up, keys_head)
    return jnp.stack([grad_gate, grad_up, grad_down])

def renormalize(base, moment):
    updated = base - moment
    base_rms = jnp.sqrt(lax.optimization_barrier(jnp.mean(base * base, axis=-1, keepdims=True)) + NORM_EPS)
    new_rms = jnp.sqrt(lax.optimization_barrier(jnp.mean(updated * updated, axis=-1, keepdims=True)) + NORM_EPS)
    return (updated * (base_rms / new_rms)).astype(jnp.bfloat16)

def fast_output(queries_head, renewed):
    h_gate = times_transposed(queries_head, renewed[0])
    h_up = times_transposed(queries_head, renewed[1])
    fast_in = (h_gate * jax.nn.sigmoid(h_gate) * h_up).astype(jnp.bfloat16)
    return times_transposed(fast_in, renewed[2])

def window_attention(queries_head, keys_head, values_head):
    total = queries_head.shape[0]
    block = math.gcd(512, total)
    padding = jnp.zeros((WINDOW, HD), jnp.bfloat16)
    padded_keys = jnp.concatenate([padding, keys_head], axis=0)
    padded_values = jnp.concatenate([padding, values_head], axis=0)

    def one_block(start):
        q_block = lax.dynamic_slice_in_dim(queries_head, start, block, 0)
        k_block = lax.dynamic_slice_in_dim(padded_keys, start, block + WINDOW, 0)
        v_block = lax.dynamic_slice_in_dim(padded_values, start, block + WINDOW, 0)
        q_pos = start + jnp.arange(block).astype(jnp.int32)
        k_pos = start - WINDOW + jnp.arange(block + WINDOW).astype(jnp.int32)
        spacing = q_pos[:, None] - k_pos[None, :]
        allowed = (spacing >= 0) & (spacing < WINDOW) & (k_pos[None, :] >= 0)
        scores = times_transposed(q_block, k_block) * (1.0 / math.sqrt(HD))
        scores = jnp.where(allowed, scores, NEG_LARGE)
        highest = lax.optimization_barrier(jnp.max(scores, axis=1, keepdims=True))
        expo = jnp.exp(scores - highest)
        probs = (expo / lax.optimization_barrier(jnp.sum(expo, axis=1, keepdims=True))).astype(jnp.bfloat16)
        return jnp.dot(probs, v_block, preferred_element_type=jnp.float32)
    starts = (jnp.arange(total // block) * block).astype(jnp.int32)
    return lax.map(one_block, starts).reshape(total, HD)

def reference(queries, keys, values, rates, fast, momentum, out_proj):
    grad_scale = 1.0 / math.sqrt(TOKENS)
    pieces = []
    moments = []
    for head_number in range(HEADS):
        first = head_number * HD
        q_head = queries[:, first:first + HD]
        k_head = keys[:, first:first + HD]
        v_head = values[:, first:first + HD]
        grads = fast_gradients(k_head, v_head, rates[:, head_number:head_number + 1], fast[head_number], grad_scale)
        moment = MOMENTUM_DECAY * momentum[head_number] + grads
        renewed = renormalize(fast[head_number].astype(jnp.float32), moment)
        fast_out = fast_output(q_head, renewed)
        attended = window_attention(q_head, k_head, v_head)
        pieces.append((attended + fast_out).astype(jnp.bfloat16))
        moments.append(moment)
    combined = jnp.concatenate(pieces, axis=1)
    mixed = jnp.dot(combined, out_proj, preferred_element_type=jnp.float32).astype(jnp.bfloat16)
    return (mixed, jnp.stack(moments))
```

```python
import functools
import math

import jax
import jax.numpy as jnp
from jax import lax
from jax.experimental import pallas as pl
from jax.experimental.pallas import tpu as pltpu
from jax.sharding import PartitionSpec as P

MOMENTUM_DECAY = 0.9
NORM_EPS = 1e-06
NEG_LARGE = -1e30
LANES = 128
MESH = pl.DeviceIdType.MESH
F32 = jnp.float32
BF16 = jnp.bfloat16


def nt(left, right):
    return lax.dot_general(left, right, (((1,), (1,)), ((), ())), preferred_element_type=F32)


def nn(left, right):
    return lax.dot_general(left, right, (((1,), (0,)), ((), ())), preferred_element_type=F32)


def tn(left, right):
    return lax.dot_general(left, right, (((0,), (0,)), ((), ())), preferred_element_type=F32)


def layer_kernel(
    side, heads, grad_scale,
    q_hbm, k_hbm, v_hbm, rates_ref, fast_hbm, mom_ref, proj_hbm,
    out_ref, newmom_ref,
    q_ref, fast_ref, ext_k, ext_v, err_t, grads, gbuf, exbuf, s1buf, r1buf, s2buf, r2buf,
    fin, sibfin, mompad, sibmom, rbuf, renewed, wbuf, wnat, att, comb, acc,
    load_sem, ex_send, ex_recv, kv_send, kv_recv, mom_send, mom_recv,
    a_send, a_recv, b_send, b_recv, fin_send, fin_recv,
    g1_send, g1_recv, g2_send, g2_recv, gs_send, gs_recv,
    w1_send, w1_recv, w2_send, w2_recv, ws_send, ws_recv,
    x_send, x_recv, f_send, f_recv,
):
    tok = q_ref.shape[0]
    hd = q_ref.shape[1]
    half = hd // 2
    blocks = half // LANES
    chips = side * side
    rows = hd // chips
    own_rows = rows // 2
    tall = rows * blocks

    seq = lax.axis_index("seq")
    head = lax.axis_index("head")
    core = lax.rem(seq, 2)
    chip = lax.div(seq, 2)
    y = lax.div(chip, side)
    z = lax.rem(chip, side)
    a1 = y + core * (z - y)
    a2 = z + core * (y - z)
    ranks = 2 * chips

    def along(d, first):
        use_y = (1 - core) if first else core
        py = lax.rem(y + d * use_y, side)
        pz = lax.rem(z + d * (1 - use_y), side)
        return ((py * side + pz) * 2 + core, head)

    def coord(d, first):
        return lax.rem((a1 if first else a2) + d, side)

    sibling = (chip * 2 + 1 - core, head)
    after = (lax.rem(seq + 1, ranks), head)
    right = (seq, lax.rem(head + 1, heads))
    left = (seq, lax.rem(head + heads - 1, heads))
    far = (lax.rem(seq + 2 * core - 1 + ranks, ranks), head)

    def remote(src, dst, send, recv, device):
        return pltpu.make_async_remote_copy(
            src_ref=src, dst_ref=dst, send_sem=send, recv_sem=recv,
            device_id=device, device_id_type=MESH,
        )

    barrier = pltpu.get_barrier_semaphore()

    def greet(d, _):
        pl.semaphore_signal(barrier, inc=1, device_id=along(d, True), device_id_type=MESH)
        pl.semaphore_signal(barrier, inc=1, device_id=along(d, False), device_id_type=MESH)
        return 0

    lax.fori_loop(1, side, greet, 0)
    for device in (sibling, right, left, far):
        pl.semaphore_signal(barrier, inc=1, device_id=device, device_id_type=MESH)

    loads = [
        pltpu.make_async_copy(k_hbm, ext_k.at[pl.ds(tok, tok)], load_sem.at[0]),
        pltpu.make_async_copy(fast_hbm, fast_ref, load_sem.at[1]),
        pltpu.make_async_copy(v_hbm, ext_v.at[pl.ds(tok, tok)], load_sem.at[2]),
        pltpu.make_async_copy(q_hbm, q_ref, load_sem.at[3]),
        pltpu.make_async_copy(proj_hbm, wbuf.at[core, a1, a2], load_sem.at[4]),
    ]
    for load in loads:
        load.start()

    row_of = lax.broadcasted_iota(jnp.int32, (rows, hd), 0)
    for m in range(3):
        padded = jnp.zeros((rows, hd), F32)
        for r in range(own_rows):
            value = MOMENTUM_DECAY * mom_ref[0, m, r:r + 1, :]
            padded = jnp.where(row_of == r + own_rows * core, jnp.broadcast_to(value, (rows, hd)), padded)
        mompad[m] = padded

    loads[2].wait()
    rate_row = -grad_scale * rates_ref[...]
    err_t[...] = (rate_row * ext_v[tok:, :].astype(F32).T).astype(BF16)
    loads[0].wait()
    loads[1].wait()
    hid = min(256, hd)

    def gradient(i, _):
        part = pl.ds(pl.multiple_of(i * hid, hid), hid)
        keys = ext_k[tok:, :]
        gate = nt(fast_ref[0, 0, part, :], keys)
        up = nt(fast_ref[0, 1, part, :], keys)
        sigma = jax.nn.sigmoid(gate)
        gated = (gate * sigma * up).astype(BF16)
        back = tn(fast_ref[0, 2, :, part], err_t[...])
        d_gate = (back * up * sigma * (1.0 + gate * (1.0 - sigma))).astype(BF16)
        d_up = (back * gate * sigma).astype(BF16)
        grads[0, part, :] = nn(d_gate, keys)
        grads[1, part, :] = nn(d_up, keys)
        grads[2, :, part] = nt(err_t[...], gated)
        return 0

    lax.fori_loop(0, hd // hid, gradient, 0)

    def pack(i, _):
        m = lax.div(i, side)
        py = lax.rem(i, side)
        line = grads[m, pl.ds(pl.multiple_of(py * side * rows, side * rows), side * rows), :]
        line = line.reshape(side, rows, hd)
        for h in range(2):
            pieces = [
                line[:, :, h * half + b * LANES:h * half + (b + 1) * LANES] for b in range(blocks)
            ]
            tile = (jnp.concatenate(pieces, axis=1) if blocks > 1 else pieces[0]).astype(BF16)
            if h == 0:
                gbuf[0, m, py] = tile
            else:
                gbuf[1, m, :, py] = tile
        return 0

    lax.fori_loop(0, 3 * side, pack, 0)

    pl.semaphore_wait(barrier, 2 * (side - 1) + 4)

    exchange = [
        remote(gbuf.at[1 - core, m], exbuf.at[m], ex_send.at[m], ex_recv.at[m], sibling)
        for m in range(3)
    ]
    for copy in exchange:
        copy.start()
    mom_copy = remote(mompad, sibmom, mom_send, mom_recv, sibling)
    mom_copy.start()

    def stage_a(m, d):
        return remote(
            s1buf.at[m, coord(d, True)], r1buf.at[m, d - 1],
            a_send.at[m, d - 1], a_recv.at[m, d - 1], along(d, True),
        )

    def stage_b(d):
        return remote(
            s2buf.at[coord(d, False)], r2buf.at[d - 1],
            b_send.at[d - 1], b_recv.at[d - 1], along(d, False),
        )

    def each(fn):
        lax.fori_loop(1, side, lambda d, _: (fn(d), 0)[1], 0)

    for m in range(3):
        exchange[m].wait_recv()
        s1buf[m] = (gbuf[core, m].astype(F32) + exbuf[m].astype(F32)).astype(BF16)
        each(lambda d, m=m: stage_a(m, d).start())

    loads[4].wait()

    def w_first(d):
        spot = wbuf.at[core, a1, a2]
        return remote(spot, spot, w1_send.at[d - 1], w1_recv.at[d - 1], along(d, False))

    def w_second(d):
        slab = wbuf.at[core, a1]
        return remote(slab, slab, w2_send.at[d - 1], w2_recv.at[d - 1], along(d, True))

    each(lambda d: w_first(d).start())
    kv = [
        remote(ext.at[pl.ds(tok, tok)], ext.at[pl.ds(0, tok)], kv_send.at[i], kv_recv.at[i], after)
        for i, ext in enumerate((ext_k, ext_v))
    ]
    for copy in kv:
        copy.start()

    for m in range(3):
        each(lambda d, m=m: stage_a(m, d).wait_recv())
        total = s1buf[m, a1].astype(F32)
        for d in range(side - 1):
            total = total + r1buf[m, d].astype(F32)
        s2buf[:, m] = total.astype(BF16)
    each(lambda d: stage_b(d).start())
    each(lambda d: stage_b(d).wait_recv())
    total = s2buf[a2].astype(F32)
    for d in range(side - 1):
        total = total + r2buf[d].astype(F32)
    fin[...] = total
    fin_copy = remote(fin, sibfin, fin_send, fin_recv, sibling)
    fin_copy.start()
    mom_copy.wait_recv()
    fin_copy.wait_recv()

    pair = max(1, 16 // rows)
    base_row = pl.multiple_of(lax.div(chip, pair) * (pair * rows), pair * rows)
    for m in range(3):
        mine, other = fin[m], sibfin[m]
        lanes = []
        for h in range(2):
            use = jnp.where(core == h, mine, other)
            lanes += [use[b * rows:(b + 1) * rows] for b in range(blocks)]
        moment = jnp.concatenate(lanes, axis=1) + (mompad[m] + sibmom[m])
        for r in range(own_rows):
            newmom_ref[0, m, r:r + 1, :] = jnp.where(
                core == 0, moment[r:r + 1], moment[own_rows + r:own_rows + r + 1]
            )
        wide = fast_ref[0, m, pl.ds(base_row, pair * rows), :].astype(F32)
        base = wide[:rows]
        for p in range(1, pair):
            base = jnp.where(lax.rem(chip, pair) == p, wide[p * rows:(p + 1) * rows], base)
        updated = base - moment
        base_rms = jnp.sqrt(jnp.mean(base * base, axis=-1, keepdims=True) + NORM_EPS)
        new_rms = jnp.sqrt(jnp.mean(updated * updated, axis=-1, keepdims=True) + NORM_EPS)
        fresh = updated * (base_rms / new_rms)
        fresh = jnp.where(core == 0, fresh[:, :half], fresh[:, half:])
        parts = [fresh[:, b * LANES:(b + 1) * LANES] for b in range(blocks)]
        packed = jnp.concatenate(parts, axis=0) if blocks > 1 else parts[0]
        rbuf[core, a1, a2, m] = packed.astype(BF16)

    def g_first(d):
        spot = rbuf.at[core, a1, a2]
        return remote(spot, spot, g1_send.at[d - 1], g1_recv.at[d - 1], along(d, False))

    def g_second(d):
        slab = rbuf.at[core, a1]
        return remote(slab, slab, g2_send.at[d - 1], g2_recv.at[d - 1], along(d, True))

    def g_sib(d):
        slab = rbuf.at[core, coord(side - d, True)]
        return remote(slab, slab, gs_send.at[d], gs_recv.at[d], sibling)

    each(lambda d: g_first(d).start())
    each(lambda d: g_first(d).wait_recv())
    each(lambda d: g_second(d).start())
    g_sib(0).start()

    each(lambda d: w_first(d).wait_recv())
    each(lambda d: w_second(d).start())

    loads[3].wait()
    for copy in kv:
        copy.wait_recv()
    chunk = tok // 4
    span = tok + chunk
    scale = 1.0 / math.sqrt(hd)
    q_local = lax.broadcasted_iota(jnp.int32, (chunk, span), 0)
    k_local = lax.broadcasted_iota(jnp.int32, (chunk, span), 1)
    window = (k_local > q_local) & (k_local <= q_local + tok)

    def attend(i, _):
        part = pl.ds(pl.multiple_of(i * chunk, chunk), chunk)
        reach = pl.ds(pl.multiple_of(i * chunk, chunk), span)
        first_key = jnp.where(seq == 0, tok, 0) - i * chunk
        scores = nt(q_ref[part, :], ext_k[reach, :]) * scale
        scores = jnp.where(window & (k_local >= first_key), scores, NEG_LARGE)
        highest = jnp.max(scores, axis=1, keepdims=True)
        expo = jnp.exp(scores - highest)
        total = jnp.sum(expo, axis=1, keepdims=True)
        att[part, :] = nn(expo.astype(BF16), ext_v[reach, :]) / total
        return 0

    lax.fori_loop(0, 4, attend, 0)

    def relay(d):
        g_second(d).wait_recv()
        g_sib(d).start()

    each(relay)
    lax.fori_loop(0, side, lambda d, _: (g_sib(d).wait_recv(), 0)[1], 0)

    def unpack(py, _):
        for m in range(3):
            lanes = []
            for h in range(2):
                tile = (rbuf[0, py, :, m] if h == 0 else rbuf[1, :, py, m]).astype(F32)
                lanes += [
                    tile[:, b * rows:(b + 1) * rows].reshape(side * rows, LANES) for b in range(blocks)
                ]
            place = pl.ds(pl.multiple_of(py * side * rows, side * rows), side * rows)
            renewed[m, place, :] = jnp.concatenate(lanes, axis=1).astype(BF16)
        return 0

    lax.fori_loop(0, side, unpack, 0)

    def to_right(i):
        piece = comb.at[head, pl.ds(pl.multiple_of(i * chunk, chunk), chunk)]
        return remote(piece, piece, x_send.at[0, i], x_recv.at[0, i], right)

    def to_left(i):
        piece = comb.at[head, pl.ds(pl.multiple_of(i * chunk, chunk), chunk)]
        return remote(piece, piece, x_send.at[1, i], x_recv.at[1, i], left)

    def forward(i, way):
        source = lax.rem(head + (heads - 1 if way == 0 else 1), heads)
        piece = comb.at[source, pl.ds(pl.multiple_of(i * chunk, chunk), chunk)]
        return remote(piece, piece, f_send.at[i], f_recv.at[i], right if way == 0 else left)

    def produce(n, _):
        i = 2 * lax.rem(n, 2) + lax.div(n, 2)
        part = pl.ds(pl.multiple_of(i * chunk, chunk), chunk)
        gate = nt(q_ref[part, :], renewed[0])
        up = nt(q_ref[part, :], renewed[1])
        fast_in = (gate * jax.nn.sigmoid(gate) * up).astype(BF16)
        fast_out = nt(fast_in, renewed[2])
        comb[head, part, :] = (att[part, :] + fast_out).astype(BF16)
        to_right(i).start()
        to_left(i).start()
        return 0

    lax.fori_loop(0, 4, produce, 0)

    each(lambda d: w_second(d).wait_recv())
    w_sib = remote(wbuf.at[core], wbuf.at[core], ws_send, ws_recv, sibling)
    w_sib.start()
    w_sib.wait_recv()
    w_rows = wbuf.shape[3]

    def natural(py, _):
        for pz in range(side):
            start = pl.multiple_of((py * side + pz) * 2 * w_rows, 2 * w_rows)
            wnat[pl.ds(start, w_rows), :] = wbuf[0, py, pz]
            wnat[pl.ds(start + w_rows, w_rows), :] = wbuf[1, pz, py]
        return 0

    lax.fori_loop(0, side, natural, 0)

    def project(source, i, first=False, last=False):
        part = pl.ds(pl.multiple_of(i * chunk, chunk), chunk)
        slab = wnat[pl.ds(pl.multiple_of(source * hd, hd), hd), :]
        value = nn(comb[source, part, :], slab)
        if not first:
            value = acc[part, :] + value
        if last:
            out_ref[part, :] = value.astype(BF16)
        else:
            acc[part, :] = value

    lax.fori_loop(0, 4, lambda i, _: (project(head, i, first=True), 0)[1], 0)

    from_left = lax.rem(head + heads - 1, heads)
    from_right = lax.rem(head + 1, heads)
    opposite = lax.rem(head + 2, heads)

    def neighbours(n, _):
        low = n
        high = n + 2
        to_right(low).wait_recv()
        forward(low, 0).start()
        to_left(low).wait_recv()
        project(from_left, low)
        project(from_right, low)
        to_left(high).wait_recv()
        forward(high, 1).start()
        to_right(high).wait_recv()
        project(from_left, high)
        project(from_right, high)
        return 0

    lax.fori_loop(0, 2, neighbours, 0)

    def finish(n, _):
        forward(n, 0).wait_recv()
        project(opposite, n, last=True)
        forward(n + 2, 1).wait_recv()
        project(opposite, n + 2, last=True)
        return 0

    lax.fori_loop(0, 2, finish, 0)

    for copy in exchange + kv + [mom_copy, fin_copy, w_sib]:
        copy.wait_send()

    def drain(d):
        for m in range(3):
            stage_a(m, d).wait_send()
        stage_b(d).wait_send()
        g_first(d).wait_send()
        g_second(d).wait_send()
        w_first(d).wait_send()
        w_second(d).wait_send()

    each(drain)
    lax.fori_loop(0, side, lambda d, _: (g_sib(d).wait_send(), 0)[1], 0)

    def drain_x(n, _):
        for i in (n, n + 2):
            to_right(i).wait_send()
            to_left(i).wait_send()
        forward(n, 0).wait_send()
        forward(n + 2, 1).wait_send()
        return 0

    lax.fori_loop(0, 2, drain_x, 0)


def shards(side, queries, keys, values, rates, fast, momentum, out_proj):
    tok, hd = queries.shape
    heads = lax.axis_size("head")
    ranks = lax.axis_size("seq")
    half = hd // 2
    blocks = half // LANES
    rows = hd // (side * side)
    tall = rows * blocks
    w_rows = out_proj.shape[0]
    grad_scale = 1.0 / math.sqrt(tok * ranks)
    dma = pltpu.SemaphoreType.DMA
    peers = side - 1
    anywhere = pl.BlockSpec(memory_space=pl.ANY)
    vmem = pl.BlockSpec(memory_space=pltpu.VMEM)
    return tuple(pl.pallas_call(
        functools.partial(layer_kernel, side, heads, grad_scale),
        out_shape=(
            jax.ShapeDtypeStruct((tok, hd), BF16),
            jax.ShapeDtypeStruct(momentum.shape, F32),
        ),
        in_specs=[anywhere, anywhere, anywhere, vmem, anywhere, vmem, anywhere],
        out_specs=(vmem, vmem),
        scratch_shapes=[
            pltpu.VMEM((tok, hd), BF16),
            pltpu.VMEM((1, 3, hd, hd), BF16),
            pltpu.VMEM((2 * tok, hd), BF16),
            pltpu.VMEM((2 * tok, hd), BF16),
            pltpu.VMEM((hd, tok), BF16),
            pltpu.VMEM((3, hd, hd), F32),
            pltpu.VMEM((2, 3, side, side, tall, LANES), BF16),
            pltpu.VMEM((3, side, side, tall, LANES), BF16),
            pltpu.VMEM((3, side, side, tall, LANES), BF16),
            pltpu.VMEM((3, peers, side, tall, LANES), BF16),
            pltpu.VMEM((side, 3, tall, LANES), BF16),
            pltpu.VMEM((peers, 3, tall, LANES), BF16),
            pltpu.VMEM((3, tall, LANES), F32),
            pltpu.VMEM((3, tall, LANES), F32),
            pltpu.VMEM((3, rows, hd), F32),
            pltpu.VMEM((3, rows, hd), F32),
            pltpu.VMEM((2, side, side, 3, tall, LANES), BF16),
            pltpu.VMEM((3, hd, hd), BF16),
            pltpu.VMEM((2, side, side, w_rows, hd), BF16),
            pltpu.VMEM((heads * hd, hd), BF16),
            pltpu.VMEM((tok, hd), F32),
            pltpu.VMEM((heads, tok, hd), BF16),
            pltpu.VMEM((tok, hd), F32),
            dma((5,)), dma((3,)), dma((3,)), dma((2,)), dma((2,)), dma(()), dma(()),
            dma((3, peers)), dma((3, peers)), dma((peers,)), dma((peers,)), dma(()), dma(()),
            dma((peers,)), dma((peers,)), dma((peers,)), dma((peers,)), dma((side,)), dma((side,)),
            dma((peers,)), dma((peers,)), dma((peers,)), dma((peers,)), dma(()), dma(()),
            dma((2, 4)), dma((2, 4)), dma((4,)), dma((4,)),
        ],
        compiler_params=pltpu.CompilerParams(
            collective_id=0, has_side_effects=True, vmem_limit_bytes=56 * 1024 * 1024,
        ),
    )(queries, keys, values, rates.reshape(1, tok), fast, momentum, out_proj))


def solution(mesh):
    side = math.isqrt(mesh.shape["seq"] // 2)
    return jax.shard_map(
        functools.partial(shards, side),
        mesh=mesh,
        in_specs=(
            P("seq", "head"),
            P("seq", "head"),
            P("seq", "head"),
            P("seq", "head"),
            P("head", None, None, None),
            P("head", None, "seq", None),
            P("seq", "head"),
        ),
        out_specs=(P("seq", "head"), P("head", None, "seq", None)),
        check_vma=False,
    )
```

```python
import functools
import math

import jax
import jax.numpy as jnp
from jax import lax
from jax.experimental import pallas as pl
from jax.experimental.pallas import tpu as pltpu
from jax.sharding import PartitionSpec as P

MOMENTUM_DECAY = 0.9
NORM_EPS = 1e-06
NEG_LARGE = -1e30
LANES = 128
MESH = pl.DeviceIdType.MESH
F32 = jnp.float32
BF16 = jnp.bfloat16


def nt(left, right):
    return lax.dot_general(left, right, (((1,), (1,)), ((), ())), preferred_element_type=F32)


def nn(left, right):
    return lax.dot_general(left, right, (((1,), (0,)), ((), ())), preferred_element_type=F32)


def tn(left, right):
    return lax.dot_general(left, right, (((0,), (0,)), ((), ())), preferred_element_type=F32)


def layer_kernel(
    side, heads, grad_scale,
    q_hbm, k_hbm, v_hbm, rates_hbm, fast_hbm, mom_hbm, proj_hbm,
    out_ref, newmom_ref,
    rates_ref, mom_ref, q_ref, fast_ref, ext_k, ext_v, err_t, grads, gbuf, exbuf, s1buf, r1buf, rhalf, aggbuf, s2buf, r2buf,
    r2sib, mompad, sibmom, rbuf, renewed, wbuf, wnat, att, comb, acc,
    load_sem, ex_send, ex_recv, kv_send, kv_recv, mom_send, mom_recv,
    a_send, a_recv, b_send, b_recv, c_send, c_recv,
    g1_send, g1_recv, g2_send, g2_recv, gs_send, gs_recv,
    w1_send, w1_recv, w2_send, w2_recv, ws_send, ws_recv,
    x_send, x_recv, f_send, f_recv,
):
    tok = q_ref.shape[0]
    hd = q_ref.shape[1]
    half = hd // 2
    blocks = half // LANES
    chips = side * side
    rows = hd // chips
    own_rows = rows // 2
    tall = rows * blocks

    seq = lax.axis_index("seq")
    head = lax.axis_index("head")
    core = lax.rem(seq, 2)
    chip = lax.div(seq, 2)
    y = lax.div(chip, side)
    z = lax.rem(chip, side)
    a1 = y + core * (z - y)
    a2 = z + core * (y - z)
    ranks = 2 * chips

    def along(d, first, swap=False):
        use_y = (1 - core) if first else core
        py = lax.rem(y + d * use_y, side)
        pz = lax.rem(z + d * (1 - use_y), side)
        return ((py * side + pz) * 2 + (1 - core if swap else core), head)

    sibling = (chip * 2 + 1 - core, head)
    after = (lax.rem(seq + 1, ranks), head)
    right = (seq, lax.rem(head + 1, heads))
    left = (seq, lax.rem(head + heads - 1, heads))
    far = (lax.rem(seq + 2 * core - 1 + ranks, ranks), head)

    def remote(src, dst, send, recv, device):
        return pltpu.make_async_remote_copy(
            src_ref=src, dst_ref=dst, send_sem=send, recv_sem=recv,
            device_id=device, device_id_type=MESH,
        )

    loads = [
        pltpu.make_async_copy(k_hbm, ext_k.at[pl.ds(tok, tok)], load_sem.at[0]),
        pltpu.make_async_copy(fast_hbm, fast_ref, load_sem.at[1]),
        pltpu.make_async_copy(v_hbm, ext_v.at[pl.ds(tok, tok)], load_sem.at[2]),
        pltpu.make_async_copy(q_hbm, q_ref, load_sem.at[3]),
        pltpu.make_async_copy(proj_hbm, wbuf.at[core, a1, a2], load_sem.at[4]),
        pltpu.make_async_copy(mom_hbm, mom_ref, load_sem.at[5]),
        pltpu.make_async_copy(rates_hbm, rates_ref, load_sem.at[6]),
    ]
    for load in (loads[0], loads[1], loads[2], loads[6], loads[5], loads[4], loads[3]):
        load.start()

    barrier = pltpu.get_barrier_semaphore()

    def greet(d, _):
        for first in (True, False):
            for swap in (True, False):
                device = along(d, first, swap)
                pl.semaphore_signal(barrier, inc=1, device_id=device, device_id_type=MESH)
        return 0

    lax.fori_loop(1, side, greet, 0)
    for device in (sibling, right, left, far):
        pl.semaphore_signal(barrier, inc=1, device_id=device, device_id_type=MESH)

    for load in (loads[0], loads[1], loads[2], loads[6]):
        load.wait()

    def gradient(i, first):
        part = pl.ds(pl.multiple_of(i * half, half), half)
        keys = ext_k[tok:, :]
        gate = nt(fast_ref[0, 0, part, :], keys)
        up = nt(fast_ref[0, 1, part, :], keys)
        if first:
            rate_row = -grad_scale * rates_ref[...]
            err_t[...] = (rate_row * ext_v[tok:, :].astype(F32).T).astype(BF16)
        sigma = jax.nn.sigmoid(gate)
        gated = (gate * sigma * up).astype(BF16)
        back = tn(fast_ref[0, 2, :, part], err_t[...])
        grads[2, :, part] = nt(err_t[...], gated)
        d_gate = (back * up * sigma * (1.0 + gate * (1.0 - sigma))).astype(BF16)
        d_up = (back * gate * sigma).astype(BF16)
        grads[0, part, :] = nn(d_gate, keys)
        grads[1, part, :] = nn(d_up, keys)

    def pieces_of(m, py, h):
        line = grads[m, pl.ds(pl.multiple_of(py * side * rows, side * rows), side * rows), h * half:(h + 1) * half]
        line = line.reshape(side, rows, half)
        parts = [line[:, :, b * LANES:(b + 1) * LANES] for b in range(blocks)]
        tile = (jnp.concatenate(parts, axis=1) if blocks > 1 else parts[0]).astype(BF16)
        if h == 0:
            gbuf[0, m, py] = tile
        else:
            gbuf[1, m, :, py] = tile

    def pack_rows(i):
        def body(n, _):
            for m in range(2):
                for h in range(2):
                    pieces_of(m, i * (side // 2) + n, h)
            return 0

        lax.fori_loop(0, side // 2, body, 0)

    def pack_down(i):
        for h in range(2):
            @pl.when(i == h)
            def _():
                lax.fori_loop(0, side, lambda n, _: (pieces_of(2, n, h), 0)[1], 0)

    def ex_down():
        return remote(gbuf.at[1 - core, 2], exbuf.at[2], ex_send.at[4], ex_recv.at[4], sibling)

    def ex_part(m, p, c):
        where = (1 - c, m, pl.ds(p * (side // 2), side // 2))
        if c == 0:
            where = (1 - c, m, slice(None), pl.ds(p * (side // 2), side // 2))
        return remote(
            gbuf.at[where], exbuf.at[where[1:]], ex_send.at[2 * m + p], ex_recv.at[2 * m + p], sibling
        )

    def ex_parts(mine):
        for c in range(2):
            p = c if mine else 1 - c

            @pl.when(core == c)
            def _():
                for m in range(2):
                    ex_part(m, p, c).start()

    def each(fn):
        lax.fori_loop(1, side, lambda d, _: (fn(d), 0)[1], 0)

    def w_first(d):
        spot = wbuf.at[core, a1, a2]
        return remote(spot, spot, w1_send.at[d - 1], w1_recv.at[d - 1], along(d, False))

    ways = ((side - 1, 0), (1, 1))

    def half_of(w):
        return pl.ds(w * (side // 2), side // 2)

    def coord(d, first):
        return lax.rem((a1 if first else a2) + d, side)

    def second(buf, send, recv, kind, d, w):
        back = side - d
        if kind == 0:
            slab, reach = buf.at[core, a1], 2 * d
        elif kind == 1:
            slab, reach = buf.at[core, a1], d
        elif kind == 2:
            slab, reach = buf.at[core, coord(2 * back, True)], d
        else:
            slab, reach = buf.at[core, coord(2 * back, True), half_of(w)], 2 * d
        return remote(slab, slab, send.at[kind, w], recv.at[kind, w], along(reach, True))

    def w_second(kind, d, w):
        return second(wbuf, w2_send, w2_recv, kind, d, w)

    def w_sib(n):
        slab = wbuf.at[core, coord(n, True)]
        return remote(slab, slab, ws_send.at[n], ws_recv.at[n], sibling)

    gradient(1 - core, True)
    pl.semaphore_wait(barrier, 4 * (side - 1) + 4)
    kv_rows = tok // 4
    kv = [
        remote(
            ext.at[pl.ds(tok + n * kv_rows, kv_rows)], ext.at[pl.ds(n * kv_rows, kv_rows)],
            kv_send.at[i, n], kv_recv.at[i, n], after,
        )
        for i, ext in enumerate((ext_k, ext_v)) for n in range(4)
    ]
    for copy in kv[:2]:
        copy.start()
    loads[4].wait()
    each(lambda d: w_first(d).start())
    pack_down(1 - core)
    pack_rows(1 - core)
    ex_down().start()
    ex_parts(False)
    gradient(core, False)

    pack_rows(core)
    ex_parts(True)
    pack_down(core)
    loads[5].wait()
    row_of = lax.broadcasted_iota(jnp.int32, (rows, hd), 0)
    for m in range(3):
        padded = jnp.zeros((rows, hd), F32)
        for r in range(own_rows):
            value = MOMENTUM_DECAY * mom_ref[0, m, r:r + 1, :]
            padded = jnp.where(row_of == r + own_rows * core, jnp.broadcast_to(value, (rows, hd)), padded)
        mompad[m] = padded

    mom_copy = remote(mompad, sibmom, mom_send, mom_recv, sibling)
    mom_copy.start()

    def a_relay(m, d, w):
        return remote(
            s1buf.at[m, coord(3 * d, True)], r1buf.at[m, w, 0],
            a_send.at[m, w, 0], a_recv.at[m, w, 0], along(d, True),
        )

    def a_half(m, d, w):
        return remote(
            s1buf.at[m, coord(side // 2, True), half_of(w)], rhalf.at[m, w],
            a_send.at[m, w, 1], a_recv.at[m, w, 1], along(2 * d, True),
        )

    def a_direct(m, d, w):
        return remote(
            s1buf.at[m, coord(d, True)], r1buf.at[m, w, 1],
            a_send.at[m, w, 2], a_recv.at[m, w, 2], along(d, True),
        )

    def a_agg(m, d, w):
        return remote(
            aggbuf.at[m, w], r1buf.at[m, w, 2],
            a_send.at[m, w, 3], a_recv.at[m, w, 3], along(2 * d, True),
        )

    def stage_b(d, swap):
        send, recv = (c_send, c_recv) if swap else (b_send, b_recv)
        return remote(
            s2buf.at[coord(d, False)], (r2sib if swap else r2buf).at[d],
            send.at[d], recv.at[d], along(d, False, swap),
        )

    order = (2, 0, 1)
    for m in order:
        if m == 2:
            ex_down().wait_recv()
        else:
            for p in range(2):
                ex_part(m, p, 1).wait_recv()
        s1buf[m] = (gbuf[core, m].astype(F32) + exbuf[m].astype(F32)).astype(BF16)
        for stage in (a_half, a_relay, a_direct):
            for d, w in ways:
                stage(m, d, w).start()

    for copy in kv[2:4]:
        copy.start()
    for m in order:
        for d, w in ways:
            a_half(m, d, w).wait_recv()
            a_relay(m, d, w).wait_recv()
            total = s1buf[m, coord(2 * d, True)].astype(F32) + r1buf[m, w, 0].astype(F32)
            aggbuf[m, w] = total.astype(BF16)
            part = half_of(w)
            total = s1buf[m, coord(2 * d, True), part].astype(F32)
            total = total + r1buf[m, w, 0, part].astype(F32) + rhalf[m, w].astype(F32)
            aggbuf[m, w, part] = total.astype(BF16)
            a_agg(m, d, w).start()
    for m in order:
        total = s1buf[m, a1].astype(F32)
        for stage, kind in ((a_direct, 1), (a_agg, 2)):
            for d, w in ways:
                stage(m, d, w).wait_recv()
                total = total + r1buf[m, w, kind].astype(F32)
        s2buf[:, m] = total.astype(BF16)
    def b_start(d):
        stage_b(d, False).start()
        stage_b(d, True).start()

    each(b_start)
    kv[4].start()
    stage_b(0, True).start()
    stage_b(0, True).wait_recv()
    each(lambda d: stage_b(d, False).wait_recv())
    each(lambda d: stage_b(d, True).wait_recv())
    mine = s2buf[a2].astype(F32)
    other = r2sib[0].astype(F32)
    for d in range(1, side):
        mine = mine + r2buf[d].astype(F32)
        other = other + r2sib[d].astype(F32)
    mom_copy.wait_recv()
    pair = max(1, 16 // rows)
    base_row = pl.multiple_of(lax.div(chip, pair) * (pair * rows), pair * rows)
    for m in range(3):
        lanes = []
        for h in range(2):
            use = jnp.where(core == h, mine[m], other[m])
            lanes += [use[b * rows:(b + 1) * rows] for b in range(blocks)]
        moment = jnp.concatenate(lanes, axis=1) + (mompad[m] + sibmom[m])
        for r in range(own_rows):
            newmom_ref[0, m, r:r + 1, :] = jnp.where(
                core == 0, moment[r:r + 1], moment[own_rows + r:own_rows + r + 1]
            )
        wide = fast_ref[0, m, pl.ds(base_row, pair * rows), :].astype(F32)
        base = wide[:rows]
        for p in range(1, pair):
            base = jnp.where(lax.rem(chip, pair) == p, wide[p * rows:(p + 1) * rows], base)
        updated = base - moment
        base_rms = jnp.sqrt(jnp.mean(base * base, axis=-1, keepdims=True) + NORM_EPS)
        new_rms = jnp.sqrt(jnp.mean(updated * updated, axis=-1, keepdims=True) + NORM_EPS)
        fresh = updated * (base_rms / new_rms)
        fresh = jnp.where(core == 0, fresh[:, :half], fresh[:, half:])
        parts = [fresh[:, b * LANES:(b + 1) * LANES] for b in range(blocks)]
        packed = jnp.concatenate(parts, axis=0) if blocks > 1 else parts[0]
        rbuf[core, a1, a2, m] = packed.astype(BF16)

    def g_first(d):
        spot = rbuf.at[core, a1, a2]
        return remote(spot, spot, g1_send.at[d - 1], g1_recv.at[d - 1], along(d, False))

    def g_second(kind, d, w):
        return second(rbuf, g2_send, g2_recv, kind, d, w)

    def g_sib(n):
        slab = rbuf.at[core, coord(n, True)]
        return remote(slab, slab, gs_send.at[n], gs_recv.at[n], sibling)

    def spread(fn):
        for kind in (0, 1):
            for d, w in ways:
                fn(kind, d, w).start()

    def relay_far(fn):
        for d, w in ways:
            fn(0, d, w).wait_recv()
            fn(3, d, w).start()
            fn(2, d, w).start()

    def hand_near(fn, sib):
        sib(0).start()
        for d, w in ways:
            sib((side - 2 * d) % side).start()
            fn(1, d, w).wait_recv()
            sib(side - d).start()

    def hand_far(fn, sib):
        for d, w in ways:
            fn(2, d, w).wait_recv()
            sib((side - 3 * d) % side).start()
        for d, w in ways:
            fn(3, d, w).wait_recv()
        sib(side // 2).start()

    def await_sib(sib):
        lax.fori_loop(0, side, lambda n, _: (sib(n).wait_recv(), 0)[1], 0)

    each(lambda d: g_first(d).start())
    kv[5].start()
    each(lambda d: g_first(d).wait_recv())
    spread(g_second)
    for copy in kv[6:]:
        copy.start()

    relay_far(g_second)
    hand_near(g_second, g_sib)
    loads[3].wait()
    for copy in kv:
        copy.wait_recv()
    chunk = tok // 4
    span = tok + chunk
    scale = 1.0 / math.sqrt(hd)
    q_local = lax.broadcasted_iota(jnp.int32, (chunk, span), 0)
    k_local = lax.broadcasted_iota(jnp.int32, (chunk, span), 1)
    window = (k_local > q_local) & (k_local <= q_local + tok)

    def attend(i, _):
        part = pl.ds(pl.multiple_of(i * chunk, chunk), chunk)
        reach = pl.ds(pl.multiple_of(i * chunk, chunk), span)
        first_key = jnp.where(seq == 0, tok, 0) - i * chunk
        scores = nt(q_ref[part, :], ext_k[reach, :]) * scale
        scores = jnp.where(window & (k_local >= first_key), scores, NEG_LARGE)
        highest = jnp.max(scores, axis=1, keepdims=True)
        expo = jnp.exp(scores - highest)
        total = jnp.sum(expo, axis=1, keepdims=True)
        att[part, :] = nn(expo.astype(BF16), ext_v[reach, :]) / total
        return 0

    lax.fori_loop(0, 4, attend, 0)

    hand_far(g_second, g_sib)
    each(lambda d: w_first(d).wait_recv())
    spread(w_second)
    await_sib(g_sib)

    def unpack(py, _):
        for m in range(3):
            lanes = []
            for h in range(2):
                tile = (rbuf[0, py, :, m] if h == 0 else rbuf[1, :, py, m]).astype(F32)
                lanes += [
                    tile[:, b * rows:(b + 1) * rows].reshape(side * rows, LANES) for b in range(blocks)
                ]
            place = pl.ds(pl.multiple_of(py * side * rows, side * rows), side * rows)
            renewed[m, place, :] = jnp.concatenate(lanes, axis=1).astype(BF16)
        return 0

    lax.fori_loop(0, side, unpack, 0)

    def to_right(i):
        piece = comb.at[head, pl.ds(pl.multiple_of(i * chunk, chunk), chunk)]
        return remote(piece, piece, x_send.at[0, i], x_recv.at[0, i], right)

    def to_left(i):
        piece = comb.at[head, pl.ds(pl.multiple_of(i * chunk, chunk), chunk)]
        return remote(piece, piece, x_send.at[1, i], x_recv.at[1, i], left)

    def forward(i, way):
        source = lax.rem(head + (heads - 1 if way == 0 else 1), heads)
        piece = comb.at[source, pl.ds(pl.multiple_of(i * chunk, chunk), chunk)]
        return remote(piece, piece, f_send.at[i], f_recv.at[i], right if way == 0 else left)

    def produce(n, _):
        i = 2 * lax.rem(n, 2) + lax.div(n, 2)
        part = pl.ds(pl.multiple_of(i * chunk, chunk), chunk)
        gate = nt(q_ref[part, :], renewed[0])
        up = nt(q_ref[part, :], renewed[1])
        fast_in = (gate * jax.nn.sigmoid(gate) * up).astype(BF16)
        fast_out = nt(fast_in, renewed[2])
        comb[head, part, :] = (att[part, :] + fast_out).astype(BF16)
        to_right(i).start()
        to_left(i).start()
        return 0

    lax.fori_loop(0, 4, produce, 0)

    def pass_on(n):
        to_right(n).wait_recv()
        forward(n, 0).start()
        to_left(n + 2).wait_recv()
        forward(n + 2, 1).start()

    relay_far(w_second)
    hand_near(w_second, w_sib)
    pass_on(0)
    hand_far(w_second, w_sib)
    await_sib(w_sib)
    pass_on(1)
    w_rows = wbuf.shape[3]

    def natural(py, _):
        for pz in range(side):
            start = pl.multiple_of((py * side + pz) * 2 * w_rows, 2 * w_rows)
            wnat[pl.ds(start, w_rows), :] = wbuf[0, py, pz]
            wnat[pl.ds(start + w_rows, w_rows), :] = wbuf[1, pz, py]
        return 0

    lax.fori_loop(0, side, natural, 0)

    def project(source, i, first=False, last=False):
        part = pl.ds(pl.multiple_of(i * chunk, chunk), chunk)
        slab = wnat[pl.ds(pl.multiple_of(source * hd, hd), hd), :]
        value = nn(comb[source, part, :], slab)
        if not first:
            value = acc[part, :] + value
        if last:
            out_ref[part, :] = value.astype(BF16)
        else:
            acc[part, :] = value

    lax.fori_loop(0, 4, lambda i, _: (project(head, i, first=True), 0)[1], 0)

    from_left = lax.rem(head + heads - 1, heads)
    from_right = lax.rem(head + 1, heads)
    opposite = lax.rem(head + 2, heads)

    def neighbours(n, _):
        low = n
        high = n + 2
        to_left(low).wait_recv()
        project(from_left, low)
        project(from_right, low)
        to_right(high).wait_recv()
        project(from_left, high)
        project(from_right, high)
        return 0

    lax.fori_loop(0, 2, neighbours, 0)

    def finish(n, _):
        forward(n, 0).wait_recv()
        project(opposite, n, last=True)
        forward(n + 2, 1).wait_recv()
        project(opposite, n + 2, last=True)
        return 0

    lax.fori_loop(0, 2, finish, 0)

    for copy in kv + [mom_copy, ex_down()]:
        copy.wait_send()
    for m in range(2):
        for p in range(2):
            ex_part(m, p, 1).wait_send()

    def drain(d):
        stage_b(d, False).wait_send()
        stage_b(d, True).wait_send()
        g_first(d).wait_send()
        w_first(d).wait_send()

    each(drain)
    stage_b(0, True).wait_send()
    for d, w in ways:
        for m in range(3):
            for stage in (a_half, a_relay, a_direct, a_agg):
                stage(m, d, w).wait_send()
        for kind in range(4):
            g_second(kind, d, w).wait_send()
            w_second(kind, d, w).wait_send()

    def drain_sib(d, _):
        g_sib(d).wait_send()
        w_sib(d).wait_send()
        return 0

    lax.fori_loop(0, side, drain_sib, 0)

    def drain_x(n, _):
        for i in (n, n + 2):
            to_right(i).wait_send()
            to_left(i).wait_send()
        forward(n, 0).wait_send()
        forward(n + 2, 1).wait_send()
        return 0

    lax.fori_loop(0, 2, drain_x, 0)


def shards(side, queries, keys, values, rates, fast, momentum, out_proj):
    tok, hd = queries.shape
    heads = lax.axis_size("head")
    ranks = lax.axis_size("seq")
    half = hd // 2
    blocks = half // LANES
    rows = hd // (side * side)
    tall = rows * blocks
    w_rows = out_proj.shape[0]
    grad_scale = 1.0 / math.sqrt(tok * ranks)
    dma = pltpu.SemaphoreType.DMA
    peers = side - 1
    anywhere = pl.BlockSpec(memory_space=pl.ANY)
    vmem = pl.BlockSpec(memory_space=pltpu.VMEM)
    return tuple(pl.pallas_call(
        functools.partial(layer_kernel, side, heads, grad_scale),
        out_shape=(
            pltpu.VMEM((tok, hd), BF16),
            pltpu.VMEM(momentum.shape, F32),
        ),
        in_specs=[anywhere] * 7,
        out_specs=(vmem, vmem),
        scratch_shapes=[
            pltpu.VMEM((1, tok), F32),
            pltpu.VMEM(momentum.shape, F32),
            pltpu.VMEM((tok, hd), BF16),
            pltpu.VMEM((1, 3, hd, hd), BF16),
            pltpu.VMEM((2 * tok, hd), BF16),
            pltpu.VMEM((2 * tok, hd), BF16),
            pltpu.VMEM((hd, tok), BF16),
            pltpu.VMEM((3, hd, hd), F32),
            pltpu.VMEM((2, 3, side, side, tall, LANES), BF16),
            pltpu.VMEM((3, side, side, tall, LANES), BF16),
            pltpu.VMEM((3, side, side, tall, LANES), BF16),
            pltpu.VMEM((3, 2, 3, side, tall, LANES), BF16),
            pltpu.VMEM((3, 2, side // 2, tall, LANES), BF16),
            pltpu.VMEM((3, 2, side, tall, LANES), BF16),
            pltpu.VMEM((side, 3, tall, LANES), BF16),
            pltpu.VMEM((side, 3, tall, LANES), BF16),
            pltpu.VMEM((side, 3, tall, LANES), BF16),
            pltpu.VMEM((3, rows, hd), F32),
            pltpu.VMEM((3, rows, hd), F32),
            pltpu.VMEM((2, side, side, 3, tall, LANES), BF16),
            pltpu.VMEM((3, hd, hd), BF16),
            pltpu.VMEM((2, side, side, w_rows, hd), BF16),
            pltpu.VMEM((heads * hd, hd), BF16),
            pltpu.VMEM((tok, hd), F32),
            pltpu.VMEM((heads, tok, hd), BF16),
            pltpu.VMEM((tok, hd), F32),
            dma((7,)), dma((5,)), dma((5,)), dma((2, 4)), dma((2, 4)), dma(()), dma(()),
            dma((3, 2, 4)), dma((3, 2, 4)), dma((side,)), dma((side,)), dma((side,)), dma((side,)),
            dma((peers,)), dma((peers,)), dma((4, 2)), dma((4, 2)), dma((side,)), dma((side,)),
            dma((peers,)), dma((peers,)), dma((4, 2)), dma((4, 2)), dma((side,)), dma((side,)),
            dma((2, 4)), dma((2, 4)), dma((4,)), dma((4,)),
        ],
        compiler_params=pltpu.CompilerParams(
            collective_id=0, has_side_effects=True, vmem_limit_bytes=56 * 1024 * 1024,
        ),
    )(queries, keys, values, rates.reshape(1, tok), fast, momentum, out_proj))


def solution(mesh):
    side = math.isqrt(mesh.shape["seq"] // 2)
    return jax.shard_map(
        functools.partial(shards, side),
        mesh=mesh,
        in_specs=(
            P("seq", "head"),
            P("seq", "head"),
            P("seq", "head"),
            P("seq", "head"),
            P("head", None, None, None),
            P("head", None, "seq", None),
            P("seq", "head"),
        ),
        out_specs=(P("seq", "head"), P("head", None, "seq", None)),
        check_vma=False,
    )
```

```python
import functools
import math

import jax
import jax.numpy as jnp
from jax import lax
from jax.experimental import pallas as pl
from jax.experimental.pallas import tpu as pltpu
from jax.sharding import PartitionSpec as P

MOMENTUM_DECAY = 0.9
NORM_EPS = 1e-06
NEG_LARGE = -1e30
LANES = 128
MESH = pl.DeviceIdType.MESH
PLACE = {7: 0, 0: 1, 1: 2, 2: 3, 6: 4, 3: 5, 4: 6, 5: 7}
GROUPS = ((0, 3), (3, 2), (5, 3))
GROUP_STEPS = (2, 2, 3)
ACROSS = (((0, 3), None), ((3, 1), (4, 1)), (None, (5, 3)))
F32 = jnp.float32
BF16 = jnp.bfloat16


def nt(left, right):
    return lax.dot_general(left, right, (((1,), (1,)), ((), ())), preferred_element_type=F32)


def nn(left, right):
    return lax.dot_general(left, right, (((1,), (0,)), ((), ())), preferred_element_type=F32)


def tn(left, right):
    return lax.dot_general(left, right, (((0,), (0,)), ((), ())), preferred_element_type=F32)


def layer_kernel(
    side, heads, grad_scale,
    q_hbm, k_hbm, v_hbm, rates_hbm, fast_hbm, mom_hbm, proj_hbm,
    out_ref, newmom_ref,
    rates_ref, mom_ref, q_ref, fast_ref, ext_k, ext_v, err_t, grads, gbuf, exbuf, s1buf, r1buf, rhalf, aggbuf, s2buf, r2buf,
    r2sib, mompad, sibmom, rbuf, renewed, wbuf, wnat, att, comb, acc, ebuf, sums, outbuf, mombuf,
    load_sem, send_sem, ex_recv, kv_recv, mom_recv, ar_recv, ad_recv, b_recv, c_recv,
    g1_recv, gr_recv, gs_recv, w1_recv, w2_recv, ws_recv, x_recv, f_recv, out_sem,
):
    tok = q_ref.shape[0]
    hd = q_ref.shape[1]
    half = hd // 2
    blocks = half // LANES
    chips = side * side
    rows = hd // chips
    own_rows = rows // 2
    tall = rows * blocks

    seq = lax.axis_index("seq")
    head = lax.axis_index("head")
    core = lax.rem(seq, 2)
    chip = lax.div(seq, 2)
    y = lax.div(chip, side)
    z = lax.rem(chip, side)
    a1 = y + core * (z - y)
    a2 = z + core * (y - z)
    ranks = 2 * chips

    def along(d, first, swap=False):
        use_y = (1 - core) if first else core
        py = lax.rem(y + d * use_y, side)
        pz = lax.rem(z + d * (1 - use_y), side)
        return ((py * side + pz) * 2 + (1 - core if swap else core), head)

    sibling = (chip * 2 + 1 - core, head)
    after = (lax.rem(seq + 1, ranks), head)
    right = (seq, lax.rem(head + 1, heads))
    left = (seq, lax.rem(head + heads - 1, heads))
    far = (lax.rem(seq + 2 * core - 1 + ranks, ranks), head)

    def remote(src, dst, send, recv, device):
        return pltpu.make_async_remote_copy(
            src_ref=src, dst_ref=dst, send_sem=send, recv_sem=recv,
            device_id=device, device_id_type=MESH,
        )

    loads = [
        pltpu.make_async_copy(k_hbm, ext_k.at[pl.ds(tok, tok)], load_sem.at[0]),
        pltpu.make_async_copy(fast_hbm, fast_ref, load_sem.at[1]),
        pltpu.make_async_copy(v_hbm, ext_v.at[pl.ds(tok, tok)], load_sem.at[2]),
        pltpu.make_async_copy(q_hbm, q_ref, load_sem.at[3]),
        pltpu.make_async_copy(proj_hbm, wbuf.at[core, a1, a2], load_sem.at[4]),
        pltpu.make_async_copy(mom_hbm, mom_ref, load_sem.at[5]),
        pltpu.make_async_copy(rates_hbm, rates_ref, load_sem.at[6]),
    ]
    for load in (loads[0], loads[1], loads[2], loads[6], loads[5], loads[4], loads[3]):
        load.start()

    def await_bytes(ref, sem):
        remote(ref, ref, send_sem.at[0], sem, sibling).wait_recv()

    barrier = pltpu.get_barrier_semaphore()

    def greet(d, _):
        for first in (True, False):
            for swap in (True, False):
                device = along(d, first, swap)
                pl.semaphore_signal(barrier, inc=1, device_id=device, device_id_type=MESH)
        return 0

    lax.fori_loop(1, side, greet, 0)
    for device in (sibling, right, left, far):
        pl.semaphore_signal(barrier, inc=1, device_id=device, device_id_type=MESH)

    for load in (loads[0], loads[1], loads[2], loads[6]):
        load.wait()

    def gradient(i, first):
        part = pl.ds(pl.multiple_of(i * half, half), half)
        keys = ext_k[tok:, :]
        gate = nt(fast_ref[0, 0, part, :], keys)
        up = nt(fast_ref[0, 1, part, :], keys)
        if first:
            rate_row = -grad_scale * rates_ref[...]
            err_t[...] = (rate_row * ext_v[tok:, :].astype(F32).T).astype(BF16)
        sigma = jax.nn.sigmoid(gate)
        gated = (gate * sigma * up).astype(BF16)
        back = tn(fast_ref[0, 2, :, part], err_t[...])
        grads[2, :, part] = nt(err_t[...], gated)
        d_gate = (back * up * sigma * (1.0 + gate * (1.0 - sigma))).astype(BF16)
        d_up = (back * gate * sigma).astype(BF16)
        grads[0, part, :] = nn(d_gate, keys)
        grads[1, part, :] = nn(d_up, keys)

    def pieces_of(m, py, h):
        line = grads[m, pl.ds(pl.multiple_of(py * side * rows, side * rows), side * rows), h * half:(h + 1) * half]
        line = line.reshape(side, rows, half)
        parts = [line[:, :, b * LANES:(b + 1) * LANES] for b in range(blocks)]
        tile = (jnp.concatenate(parts, axis=1) if blocks > 1 else parts[0]).astype(BF16)
        if h == 0:
            gbuf[0, m, py] = tile
        else:
            gbuf[1, m, :, py] = tile

    def pack_rows(i):
        def body(n, _):
            for m in range(2):
                for h in range(2):
                    pieces_of(m, i * (side // 2) + n, h)
            return 0

        lax.fori_loop(0, side // 2, body, 0)

    def pack_down(i):
        for h in range(2):
            @pl.when(i == h)
            def _():
                lax.fori_loop(0, side, lambda n, _: (pieces_of(2, n, h), 0)[1], 0)

    def ex_down():
        return remote(gbuf.at[1 - core, 2], exbuf.at[2], send_sem.at[0], ex_recv.at[2], sibling)

    def ex_part(m, p, c):
        where = (1 - c, m, pl.ds(p * (side // 2), side // 2))
        if c == 0:
            where = (1 - c, m, slice(None), pl.ds(p * (side // 2), side // 2))
        return remote(
            gbuf.at[where], exbuf.at[where[1:]], send_sem.at[0], ex_recv.at[m], sibling
        )

    def ex_parts(mine):
        for c in range(2):
            p = c if mine else 1 - c

            @pl.when(core == c)
            def _():
                for m in range(2):
                    ex_part(m, p, c).start()

    def each(fn):
        lax.fori_loop(1, side, lambda d, _: (fn(d), 0)[1], 0)

    def w_first(d):
        spot = wbuf.at[core, a1, a2]
        return remote(spot, spot, send_sem.at[3], w1_recv, along(d, False))

    ways = ((side - 1, 0), (1, 1))

    def half_of(w):
        return pl.ds(w * (side // 2), side // 2)

    def coord(d, first):
        return lax.rem((a1 if first else a2) + d, side)

    def w_second(kind, d, w):
        buf = wbuf
        back = side - d
        if kind == 0:
            slab, reach = buf.at[core, a1], 2 * d
        elif kind == 1:
            slab, reach = buf.at[core, a1], d
        elif kind == 2:
            slab, reach = buf.at[core, coord(2 * back, True)], d
        else:
            slab, reach = buf.at[core, coord(2 * back, True), half_of(w)], 2 * d
        spot = (w, 2 + w, 4 + w, 6)[kind]
        return remote(slab, slab, send_sem.at[3], w2_recv.at[spot], along(reach, True))

    def w_sib(n):
        slab = wbuf.at[core, coord(n, True)]
        return remote(slab, slab, send_sem.at[4], ws_recv, sibling)

    gradient(1 - core, True)
    pl.semaphore_wait(barrier, 4 * (side - 1) + 4)
    kv_rows = tok // 4
    kv = [
        remote(
            ext.at[pl.ds(tok + n * kv_rows, kv_rows)], ext.at[pl.ds(n * kv_rows, kv_rows)],
            send_sem.at[1], kv_recv.at[i], after,
        )
        for i, ext in enumerate((ext_k, ext_v)) for n in range(4)
    ]
    for copy in kv[:2]:
        copy.start()
    loads[4].wait()
    each(lambda d: w_first(d).start())
    pack_down(1 - core)
    pack_rows(1 - core)
    ex_down().start()
    ex_parts(False)
    gradient(core, False)

    pack_rows(core)
    ex_parts(True)
    pack_down(core)
    loads[5].wait()
    row_of = lax.broadcasted_iota(jnp.int32, (rows, hd), 0)
    for m in range(3):
        padded = jnp.zeros((rows, hd), F32)
        for r in range(own_rows):
            value = MOMENTUM_DECAY * mom_ref[0, m, r:r + 1, :]
            padded = jnp.where(row_of == r + own_rows * core, jnp.broadcast_to(value, (rows, hd)), padded)
        mompad[m] = padded

    mom_copy = remote(mompad, sibmom, send_sem.at[0], mom_recv, sibling)
    mom_copy.start()

    def a_relay(m, d, w):
        return remote(
            s1buf.at[m, coord(3 * d, True)], r1buf.at[m, w, 0],
            send_sem.at[0], ar_recv.at[m, w], along(d, True),
        )

    def a_half(m, d, w):
        return remote(
            s1buf.at[m, coord(side // 2, True), half_of(w)], rhalf.at[m, w],
            send_sem.at[0], ar_recv.at[m, w], along(2 * d, True),
        )

    def a_direct(m, d, w):
        return remote(
            s1buf.at[m, coord(d, True)], r1buf.at[m, w, 1],
            send_sem.at[0], ad_recv.at[m], along(d, True),
        )

    def a_agg(m, d, w):
        return remote(
            aggbuf.at[m, w], r1buf.at[m, w, 2],
            send_sem.at[0], ad_recv.at[m], along(2 * d, True),
        )

    def stage_b(d, swap):
        send, recv = (send_sem.at[0], c_recv) if swap else (send_sem.at[2], b_recv)
        return remote(
            s2buf.at[coord(d, False)], (r2sib if swap else r2buf).at[d],
            send, recv, along(d, False, swap),
        )

    order = (2, 0, 1)
    for m in order:
        await_bytes(exbuf.at[m], ex_recv.at[m])
        s1buf[m] = (gbuf[core, m].astype(F32) + exbuf[m].astype(F32)).astype(BF16)
        for stage in (a_half, a_relay):
            for d, w in ways:
                stage(m, d, w).start()
    for m in order:
        for d, w in ways:
            a_direct(m, d, w).start()

    for m in order:
        for d, w in ways:
            await_bytes(rhalf.at[:, 0], ar_recv.at[m, w])
            total = s1buf[m, coord(2 * d, True)].astype(F32) + r1buf[m, w, 0].astype(F32)
            aggbuf[m, w] = total.astype(BF16)
            part = half_of(w)
            total = s1buf[m, coord(2 * d, True), part].astype(F32)
            total = total + r1buf[m, w, 0, part].astype(F32) + rhalf[m, w].astype(F32)
            aggbuf[m, w, part] = total.astype(BF16)
            a_agg(m, d, w).start()
    kv[2].start()
    for m in order:
        total = s1buf[m, a1].astype(F32)
        await_bytes(r1buf.at[m, :, pl.ds(1, 2)], ad_recv.at[m])
        for kind in (1, 2):
            for w in range(2):
                total = total + r1buf[m, w, kind].astype(F32)
        s2buf[:, m] = total.astype(BF16)
    def b_start(d):
        stage_b(d, False).start()
        stage_b(d, True).start()

    each(b_start)
    kv[3].start()
    kv[4].start()
    stage_b(0, True).start()
    await_bytes(r2buf.at[pl.ds(1, side - 1)], b_recv)
    await_bytes(r2sib, c_recv)
    mine = s2buf[a2].astype(F32)
    other = r2sib[0].astype(F32)
    for d in range(1, side):
        mine = mine + r2buf[d].astype(F32)
        other = other + r2sib[d].astype(F32)
    mom_copy.wait_recv()
    pair = max(1, 16 // rows)
    base_row = pl.multiple_of(lax.div(chip, pair) * (pair * rows), pair * rows)
    for m in range(3):
        lanes = []
        for h in range(2):
            use = jnp.where(core == h, mine[m], other[m])
            lanes += [use[b * rows:(b + 1) * rows] for b in range(blocks)]
        moment = jnp.concatenate(lanes, axis=1) + (mompad[m] + sibmom[m])
        for r in range(own_rows):
            mombuf[0, m, r:r + 1, :] = jnp.where(
                core == 0, moment[r:r + 1], moment[own_rows + r:own_rows + r + 1]
            )
        wide = fast_ref[0, m, pl.ds(base_row, pair * rows), :].astype(F32)
        base = wide[:rows]
        for p in range(1, pair):
            base = jnp.where(lax.rem(chip, pair) == p, wide[p * rows:(p + 1) * rows], base)
        updated = base - moment
        base_rms = jnp.sqrt(jnp.mean(base * base, axis=-1, keepdims=True) + NORM_EPS)
        new_rms = jnp.sqrt(jnp.mean(updated * updated, axis=-1, keepdims=True) + NORM_EPS)
        fresh = updated * (base_rms / new_rms)
        fresh = jnp.where(core == 0, fresh[:, :half], fresh[:, half:])
        parts = [fresh[:, b * LANES:(b + 1) * LANES] for b in range(blocks)]
        packed = jnp.concatenate(parts, axis=0) if blocks > 1 else parts[0]
        rbuf[core, a1, PLACE[0], m] = packed.astype(BF16)

    def g_first(d):
        return remote(
            rbuf.at[core, a1, PLACE[0]], rbuf.at[core, a1, PLACE[side - d]],
            send_sem.at[2], g1_recv.at[min(min(d, side - d), 3) - 1], along(d, False),
        )

    def g_step(g, kind, d, w):
        low, count = ACROSS[g][w] if kind == 3 else GROUPS[g]
        origin = a1 if kind < 2 else coord(2 * (side - d), True)
        reach = d if kind in (1, 2) else 2 * d
        slab = rbuf.at[core, origin, pl.ds(low, count)]
        spot = (g * 2 + w, 6 + w, 8 + w, 10)[kind]
        return remote(slab, slab, send_sem.at[1], gr_recv.at[spot], along(reach, True))

    def g_steps(kind):
        return [
            (g, kind, d, w) for g in range(3) for d, w in ways if kind < 3 or ACROSS[g][w]
        ]

    def g_sib(n):
        slab = rbuf.at[core, coord(n, True)]
        return remote(slab, slab, send_sem.at[3], gs_recv, sibling)

    def spread(fn):
        for kind in (0, 1):
            for d, w in ways:
                fn(kind, d, w).start()

    def relay_far(fn):
        for d, w in ways:
            fn(0, d, w).wait_recv()
            fn(3, d, w).start()
            fn(2, d, w).start()

    def hand_near(fn, sib):
        sib(0).start()
        for d, w in ways:
            sib((side - 2 * d) % side).start()
            fn(1, d, w).wait_recv()
            sib(side - d).start()

    def hand_far(fn, sib):
        for d, w in ways:
            fn(2, d, w).wait_recv()
            sib((side - 3 * d) % side).start()
        await_bytes(wbuf.at[0, 0], w2_recv.at[6])
        sib(side // 2).start()

    newmom_copy = pltpu.make_async_copy(mombuf, newmom_ref, out_sem.at[1])
    for d in range(1, side):
        g_first(d).start()
    kv[5].start()
    for g, steps in enumerate(GROUP_STEPS):
        low, count = (0, steps) if g else (1, steps)
        await_bytes(rbuf.at[core, a1, pl.ds(low, count)], g1_recv.at[g])
        for kind in (0, 1):
            for d, w in ways:
                g_step(g, kind, d, w).start()
    g_sib(0).start()

    newmom_copy.start()
    loads[3].wait()
    await_bytes(ext_k.at[pl.ds(0, tok)], kv_recv.at[0])
    chunk = tok // 4
    span = tok + chunk
    scale = 1.0 / math.sqrt(hd)
    q_local = lax.broadcasted_iota(jnp.int32, (chunk, span), 0)
    k_local = lax.broadcasted_iota(jnp.int32, (chunk, span), 1)
    window = (k_local > q_local) & (k_local <= q_local + tok)

    def score(i, _):
        part = pl.ds(pl.multiple_of(i * chunk, chunk), chunk)
        reach = pl.ds(pl.multiple_of(i * chunk, chunk), span)
        first_key = jnp.where(seq == 0, tok, 0) - i * chunk
        scores = nt(q_ref[part, :], ext_k[reach, :]) * scale
        scores = jnp.where(window & (k_local >= first_key), scores, NEG_LARGE)
        highest = jnp.max(scores, axis=1, keepdims=True)
        expo = jnp.exp(scores - highest)
        sums[part, :] = jnp.sum(expo, axis=1, keepdims=True)
        ebuf[i] = expo.astype(BF16)
        return 0

    lax.fori_loop(0, 4, score, 0)

    def attend(i, _):
        part = pl.ds(pl.multiple_of(i * chunk, chunk), chunk)
        reach = pl.ds(pl.multiple_of(i * chunk, chunk), span)
        att[part, :] = nn(ebuf[i], ext_v[reach, :]) / sums[part, :]
        return 0

    for g in range(3):
        for d, w in ways:
            g_step(g, 0, d, w).wait_recv()
            if ACROSS[g][w]:
                g_step(g, 3, d, w).start()
            g_step(g, 2, d, w).start()
    for copy in kv[6:]:
        copy.start()
    for d, w in ways:
        g_sib((side - 2 * d) % side).start()
    for d, w in ways:
        await_bytes(rbuf.at[0, 0], gr_recv.at[6 + w])
        g_sib(side - d).start()
    for d, w in ways:
        await_bytes(rbuf.at[0, 0], gr_recv.at[8 + w])
        g_sib((side - 3 * d) % side).start()
    await_bytes(rbuf.at[0, 0], gr_recv.at[10])
    g_sib(side // 2).start()
    await_bytes(wbuf.at[0, 0, pl.ds(0, side - 1)], w1_recv)
    spread(w_second)
    await_bytes(ext_v.at[pl.ds(0, tok)], kv_recv.at[1])
    lax.fori_loop(0, 4, attend, 0)

    def unpack(h):
        def body(py, _):
            for m in range(3):
                pieces = []
                for pz in range(side):
                    line, turn = (py, lax.rem(pz + side - z, side)) if h == 0 else (pz, lax.rem(py + side - y, side))
                    place = sum(jnp.where(turn == t, p, 0) for t, p in PLACE.items())
                    tile = rbuf[h, line, place, m].astype(F32)
                    lanes = [tile[b * rows:(b + 1) * rows] for b in range(blocks)]
                    pieces.append(jnp.concatenate(lanes, axis=1))
                part = pl.ds(pl.multiple_of(py * side * rows, side * rows), side * rows)
                renewed[m, part, h * half:(h + 1) * half] = jnp.concatenate(pieces, axis=0).astype(BF16)
            return 0

        lax.fori_loop(0, side, body, 0)

    for h in range(2):
        @pl.when(core == h)
        def _():
            unpack(h)

    await_bytes(rbuf.at[0], gs_recv)
    for h in range(2):
        @pl.when(core != h)
        def _():
            unpack(h)

    def to_right(i):
        piece = comb.at[head, pl.ds(pl.multiple_of(i * chunk, chunk), chunk)]
        return remote(piece, piece, send_sem.at[4], x_recv.at[0, i], right)

    def to_left(i):
        piece = comb.at[head, pl.ds(pl.multiple_of(i * chunk, chunk), chunk)]
        return remote(piece, piece, send_sem.at[4], x_recv.at[1, i], left)

    def forward(i, way):
        source = lax.rem(head + (heads - 1 if way == 0 else 1), heads)
        piece = comb.at[source, pl.ds(pl.multiple_of(i * chunk, chunk), chunk)]
        return remote(piece, piece, send_sem.at[5], f_recv.at[i], right if way == 0 else left)

    def produce(i, first):
        part = pl.ds(pl.multiple_of(i * chunk, chunk), chunk)
        gate = nt(q_ref[part, :], renewed[0])
        up = nt(q_ref[part, :], renewed[1])
        fast_in = (gate * jax.nn.sigmoid(gate) * up).astype(BF16)
        fast_out = nt(fast_in, renewed[2])
        comb[head, part, :] = (att[part, :] + fast_out).astype(BF16)
        if first:
            to_right(i).start()
        else:
            to_left(i).start()

    def produce_pair(n, _):
        produce(n, True)
        produce(n + 2, False)
        return 0

    lax.fori_loop(0, 2, produce_pair, 0)
    for n in range(2):
        to_right(n + 2).start()
        to_left(n).start()

    def pass_on(n):
        to_right(n).wait_recv()
        forward(n, 0).start()
        to_left(n + 2).wait_recv()
        forward(n + 2, 1).start()

    relay_far(w_second)
    hand_near(w_second, w_sib)
    pass_on(0)
    hand_far(w_second, w_sib)
    await_bytes(wbuf.at[0], ws_recv)
    pass_on(1)
    w_rows = wbuf.shape[3]

    def natural(py, _):
        for pz in range(side):
            start = pl.multiple_of((py * side + pz) * 2 * w_rows, 2 * w_rows)
            wnat[pl.ds(start, w_rows), :] = wbuf[0, py, pz]
            wnat[pl.ds(start + w_rows, w_rows), :] = wbuf[1, pz, py]
        return 0

    lax.fori_loop(0, side, natural, 0)

    def out_copy(i):
        part = pl.ds(pl.multiple_of(i * chunk, chunk), chunk)
        return pltpu.make_async_copy(outbuf.at[part], out_ref.at[part], out_sem.at[0])

    def project(source, i, first=False, last=False):
        part = pl.ds(pl.multiple_of(i * chunk, chunk), chunk)
        slab = wnat[pl.ds(pl.multiple_of(source * hd, hd), hd), :]
        value = nn(comb[source, part, :], slab)
        if not first:
            value = acc[part, :] + value
        if last:
            outbuf[part, :] = value.astype(BF16)
            out_copy(i).start()
        else:
            acc[part, :] = value

    lax.fori_loop(0, 4, lambda i, _: (project(head, i, first=True), 0)[1], 0)

    from_left = lax.rem(head + heads - 1, heads)
    from_right = lax.rem(head + 1, heads)
    opposite = lax.rem(head + 2, heads)

    def neighbours(n, _):
        low = n
        high = n + 2
        to_left(low).wait_recv()
        project(from_left, low)
        project(from_right, low)
        to_right(high).wait_recv()
        project(from_left, high)
        project(from_right, high)
        return 0

    lax.fori_loop(0, 2, neighbours, 0)

    def finish(n, _):
        forward(n, 0).wait_recv()
        project(opposite, n, last=True)
        forward(n + 2, 1).wait_recv()
        project(opposite, n + 2, last=True)
        return 0

    lax.fori_loop(0, 2, finish, 0)

    newmom_copy.wait()
    pltpu.make_async_copy(outbuf, out_ref, out_sem.at[0]).wait()
    slab = side * tall * LANES
    size = {
        0: 3 * (half * hd) + 3 * 7 * slab + side * 3 * tall * LANES + 2 * 3 * rows * hd,
        1: 2 * tok * hd + 7 * 3 * slab,
        3: 3 * side * slab + (side - 1) * w_rows * hd + 7 * side * w_rows * hd,
        4: side * side * w_rows * hd + 2 * tok * hd,
        5: tok * hd,
    }
    for n, count in size.items():
        part = wnat.at[pl.ds(0, count // hd)]
        remote(part, part, send_sem.at[n], mom_recv, sibling).wait_send()
    part = rbuf.at[0, pl.ds(0, 2), pl.ds(0, side - 1)]
    remote(part, part, send_sem.at[2], mom_recv, sibling).wait_send()


def shards(side, queries, keys, values, rates, fast, momentum, out_proj):
    tok, hd = queries.shape
    heads = lax.axis_size("head")
    ranks = lax.axis_size("seq")
    half = hd // 2
    blocks = half // LANES
    rows = hd // (side * side)
    tall = rows * blocks
    w_rows = out_proj.shape[0]
    grad_scale = 1.0 / math.sqrt(tok * ranks)
    dma = pltpu.SemaphoreType.DMA
    peers = side - 1
    anywhere = pl.BlockSpec(memory_space=pl.ANY)
    return tuple(pl.pallas_call(
        functools.partial(layer_kernel, side, heads, grad_scale),
        out_shape=(
            pltpu.VMEM((tok, hd), BF16),
            pltpu.VMEM(momentum.shape, F32),
        ),
        in_specs=[anywhere] * 7,
        out_specs=(anywhere, anywhere),
        scratch_shapes=[
            pltpu.VMEM((1, tok), F32),
            pltpu.VMEM(momentum.shape, F32),
            pltpu.VMEM((tok, hd), BF16),
            pltpu.VMEM((1, 3, hd, hd), BF16),
            pltpu.VMEM((2 * tok, hd), BF16),
            pltpu.VMEM((2 * tok, hd), BF16),
            pltpu.VMEM((hd, tok), BF16),
            pltpu.VMEM((3, hd, hd), F32),
            pltpu.VMEM((2, 3, side, side, tall, LANES), BF16),
            pltpu.VMEM((3, side, side, tall, LANES), BF16),
            pltpu.VMEM((3, side, side, tall, LANES), BF16),
            pltpu.VMEM((3, 2, 3, side, tall, LANES), BF16),
            pltpu.VMEM((3, 2, side // 2, tall, LANES), BF16),
            pltpu.VMEM((3, 2, side, tall, LANES), BF16),
            pltpu.VMEM((side, 3, tall, LANES), BF16),
            pltpu.VMEM((side, 3, tall, LANES), BF16),
            pltpu.VMEM((side, 3, tall, LANES), BF16),
            pltpu.VMEM((3, rows, hd), F32),
            pltpu.VMEM((3, rows, hd), F32),
            pltpu.VMEM((2, side, side, 3, tall, LANES), BF16),
            pltpu.VMEM((3, hd, hd), BF16),
            pltpu.VMEM((2, side, side, w_rows, hd), BF16),
            pltpu.VMEM((heads * hd, hd), BF16),
            pltpu.VMEM((tok, hd), F32),
            pltpu.VMEM((heads, tok, hd), BF16),
            pltpu.VMEM((tok, hd), F32),
            pltpu.VMEM((4, tok // 4, tok + tok // 4), BF16),
            pltpu.VMEM((tok, 1), F32),
            pltpu.VMEM((tok, hd), BF16),
            pltpu.VMEM(momentum.shape, F32),
            dma((7,)), dma((6,)), dma((3,)), dma((2,)), dma(()), dma((3, 2)), dma((3,)), dma(()), dma(()),
            dma((3,)), dma((11,)), dma(()), dma(()), dma((7,)), dma(()), dma((2, 4)), dma((4,)), dma((2,)),
        ],
        compiler_params=pltpu.CompilerParams(
            collective_id=0, has_side_effects=True, vmem_limit_bytes=56 * 1024 * 1024,
        ),
    )(queries, keys, values, rates.reshape(1, tok), fast, momentum, out_proj))


def solution(mesh):
    side = math.isqrt(mesh.shape["seq"] // 2)
    return jax.shard_map(
        functools.partial(shards, side),
        mesh=mesh,
        in_specs=(
            P("seq", "head"),
            P("seq", "head"),
            P("seq", "head"),
            P("seq", "head"),
            P("head", None, None, None),
            P("head", None, "seq", None),
            P("seq", "head"),
        ),
        out_specs=(P("seq", "head"), P("head", None, "seq", None)),
        check_vma=False,
    )
```

```python
import functools
import math

import jax
import jax.numpy as jnp
from jax import lax
from jax.experimental import pallas as pl
from jax.experimental.pallas import tpu as pltpu
from jax.sharding import PartitionSpec as P

MOMENTUM_DECAY = 0.9
NORM_EPS = 1e-06
NEG_LARGE = -1e30
LANES = 128
MESH = pl.DeviceIdType.MESH
PLACE = {7: 0, 0: 1, 1: 2, 2: 3, 6: 4, 3: 5, 4: 6, 5: 7}
GROUPS = ((0, 3), (3, 2), (5, 3))
GROUP_STEPS = (2, 2, 3)
ACROSS = (((0, 3), None), ((3, 1), (4, 1)), (None, (5, 3)))
F32 = jnp.float32
BF16 = jnp.bfloat16


def nt(left, right):
    return lax.dot_general(left, right, (((1,), (1,)), ((), ())), preferred_element_type=F32)


def nn(left, right):
    return lax.dot_general(left, right, (((1,), (0,)), ((), ())), preferred_element_type=F32)


def tn(left, right):
    return lax.dot_general(left, right, (((0,), (0,)), ((), ())), preferred_element_type=F32)


def layer_kernel(
    side, heads, grad_scale,
    q_hbm, k_hbm, v_hbm, rates_hbm, fast_hbm, mom_hbm, proj_hbm,
    out_ref, newmom_ref,
    rates_ref, mom_ref, q_ref, fast_ref, ext_k, ext_v, err_t, grads, gbuf, exbuf, s1buf, r1buf, rhalf, aggbuf, s2buf, r2buf,
    r2sib, mompad, sibmom, rbuf, renewed, wbuf, wnat, att, comb, acc, outbuf, mombuf,
    load_sem, send_sem, ex_recv, kv_recv, mom_recv, ar_recv, ad_recv, b_recv, c_recv,
    g1_recv, gr_recv, gs_recv, w1_recv, w2_recv, ws_recv, x_recv, f_recv, out_sem,
):
    tok = q_ref.shape[0]
    hd = q_ref.shape[1]
    half = hd // 2
    blocks = half // LANES
    chips = side * side
    rows = hd // chips
    own_rows = rows // 2
    tall = rows * blocks

    seq = lax.axis_index("seq")
    head = lax.axis_index("head")
    core = lax.rem(seq, 2)
    chip = lax.div(seq, 2)
    y = lax.div(chip, side)
    z = lax.rem(chip, side)
    a1 = y + core * (z - y)
    a2 = z + core * (y - z)
    ranks = 2 * chips

    def along(d, first, swap=False):
        use_y = (1 - core) if first else core
        py = lax.rem(y + d * use_y, side)
        pz = lax.rem(z + d * (1 - use_y), side)
        return ((py * side + pz) * 2 + (1 - core if swap else core), head)

    sibling = (chip * 2 + 1 - core, head)
    after = (lax.rem(seq + 1, ranks), head)
    right = (seq, lax.rem(head + 1, heads))
    left = (seq, lax.rem(head + heads - 1, heads))
    far = (lax.rem(seq + 2 * core - 1 + ranks, ranks), head)

    def remote(src, dst, send, recv, device):
        return pltpu.make_async_remote_copy(
            src_ref=src, dst_ref=dst, send_sem=send, recv_sem=recv,
            device_id=device, device_id_type=MESH,
        )

    loads = [
        pltpu.make_async_copy(k_hbm, ext_k.at[pl.ds(tok, tok)], load_sem.at[0]),
        pltpu.make_async_copy(fast_hbm.at[:, pl.ds(0, 2)], fast_ref.at[:, pl.ds(0, 2)], load_sem.at[1]),
        pltpu.make_async_copy(v_hbm, ext_v.at[pl.ds(tok, tok)], load_sem.at[2]),
        pltpu.make_async_copy(q_hbm, q_ref, load_sem.at[3]),
        pltpu.make_async_copy(proj_hbm, wbuf.at[core, a1, a2], load_sem.at[4]),
        pltpu.make_async_copy(mom_hbm, mom_ref, load_sem.at[5]),
        pltpu.make_async_copy(rates_hbm, rates_ref, load_sem.at[6]),
        pltpu.make_async_copy(fast_hbm.at[:, pl.ds(2, 1)], fast_ref.at[:, pl.ds(2, 1)], load_sem.at[7]),
    ]
    for n in (0, 1, 6, 2, 7, 5, 4, 3):
        loads[n].start()

    def await_bytes(ref, sem):
        remote(ref, ref, send_sem.at[0], sem, sibling).wait_recv()

    barrier = pltpu.get_barrier_semaphore()

    def greet(d, _):
        for first in (True, False):
            for swap in (True, False):
                device = along(d, first, swap)
                pl.semaphore_signal(barrier, inc=1, device_id=device, device_id_type=MESH)
        return 0

    lax.fori_loop(1, side, greet, 0)
    for device in (sibling, right, left, far):
        pl.semaphore_signal(barrier, inc=1, device_id=device, device_id_type=MESH)

    for n in (0, 1, 6, 2, 7):
        loads[n].wait()

    def gradient(i, first):
        part = pl.ds(pl.multiple_of(i * half, half), half)
        keys = ext_k[tok:, :]
        gate = nt(fast_ref[0, 0, part, :], keys)
        up = nt(fast_ref[0, 1, part, :], keys)
        if first:
            rate_row = -grad_scale * rates_ref[...]
            err_t[...] = (rate_row * ext_v[tok:, :].astype(F32).T).astype(BF16)
        sigma = jax.nn.sigmoid(gate)
        gated = (gate * sigma * up).astype(BF16)
        back = tn(fast_ref[0, 2, :, part], err_t[...])
        grads[2, :, part] = nt(err_t[...], gated)
        d_gate = (back * up * sigma * (1.0 + gate * (1.0 - sigma))).astype(BF16)
        d_up = (back * gate * sigma).astype(BF16)
        grads[0, part, :] = nn(d_gate, keys)
        grads[1, part, :] = nn(d_up, keys)

    def pieces_of(m, py, h):
        line = grads[m, pl.ds(pl.multiple_of(py * side * rows, side * rows), side * rows), h * half:(h + 1) * half]
        line = line.reshape(side, rows, half)
        parts = [line[:, :, b * LANES:(b + 1) * LANES] for b in range(blocks)]
        tile = (jnp.concatenate(parts, axis=1) if blocks > 1 else parts[0]).astype(BF16)
        if h == 0:
            gbuf[0, m, py] = tile
        else:
            gbuf[1, m, :, py] = tile

    def pack_rows(i):
        def body(n, _):
            for m in range(2):
                for h in range(2):
                    pieces_of(m, i * (side // 2) + n, h)
            return 0

        lax.fori_loop(0, side // 2, body, 0)

    def pack_down(i):
        for h in range(2):
            @pl.when(i == h)
            def _():
                lax.fori_loop(0, side, lambda n, _: (pieces_of(2, n, h), 0)[1], 0)

    def ex_down():
        return remote(gbuf.at[1 - core, 2], exbuf.at[2], send_sem.at[0], ex_recv.at[2], sibling)

    def ex_part(m, p, c):
        where = (1 - c, m, pl.ds(p * (side // 2), side // 2))
        if c == 0:
            where = (1 - c, m, slice(None), pl.ds(p * (side // 2), side // 2))
        return remote(
            gbuf.at[where], exbuf.at[where[1:]], send_sem.at[0], ex_recv.at[m], sibling
        )

    def ex_parts(mine):
        for c in range(2):
            p = c if mine else 1 - c

            @pl.when(core == c)
            def _():
                for m in range(2):
                    ex_part(m, p, c).start()

    def each(fn):
        lax.fori_loop(1, side, lambda d, _: (fn(d), 0)[1], 0)

    def w_first(d):
        spot = wbuf.at[core, a1, a2]
        return remote(spot, spot, send_sem.at[3], w1_recv, along(d, False))

    ways = ((side - 1, 0), (1, 1))

    def half_of(w):
        return pl.ds(w * (side // 2), side // 2)

    def coord(d, first):
        return lax.rem((a1 if first else a2) + d, side)

    def w_second(kind, d, w):
        buf = wbuf
        back = side - d
        if kind == 0:
            slab, reach = buf.at[core, a1], 2 * d
        elif kind == 1:
            slab, reach = buf.at[core, a1], d
        elif kind == 2:
            slab, reach = buf.at[core, coord(2 * back, True)], d
        else:
            slab, reach = buf.at[core, coord(2 * back, True), half_of(w)], 2 * d
        spot = (w, 2 + w, 4 + w, 6)[kind]
        return remote(slab, slab, send_sem.at[3], w2_recv.at[spot], along(reach, True))

    def w_sib(n):
        slab = wbuf.at[core, coord(n, True)]
        return remote(slab, slab, send_sem.at[4], ws_recv, sibling)

    gradient(1 - core, True)
    pl.semaphore_wait(barrier, 4 * (side - 1) + 4)
    kv_rows = tok // 4
    kv = [
        remote(
            ext.at[pl.ds(tok + n * kv_rows, kv_rows)], ext.at[pl.ds(n * kv_rows, kv_rows)],
            send_sem.at[1], kv_recv.at[i, n], after,
        )
        for n in (3, 2, 1, 0) for i, ext in enumerate((ext_k, ext_v))
    ]
    for copy in kv[:2]:
        copy.start()
    loads[4].wait()
    each(lambda d: w_first(d).start())
    pack_down(1 - core)
    pack_rows(1 - core)
    ex_down().start()
    ex_parts(False)
    gradient(core, False)

    pack_rows(core)
    ex_parts(True)
    pack_down(core)
    loads[5].wait()
    row_of = lax.broadcasted_iota(jnp.int32, (rows, hd), 0)
    for m in range(3):
        padded = jnp.zeros((rows, hd), F32)
        for r in range(own_rows):
            value = MOMENTUM_DECAY * mom_ref[0, m, r:r + 1, :]
            padded = jnp.where(row_of == r + own_rows * core, jnp.broadcast_to(value, (rows, hd)), padded)
        mompad[m] = padded

    mom_copy = remote(mompad, sibmom, send_sem.at[0], mom_recv, sibling)
    mom_copy.start()

    def a_relay(m, d, w):
        return remote(
            s1buf.at[m, coord(3 * d, True)], r1buf.at[m, w, 0],
            send_sem.at[0], ar_recv.at[m, w], along(d, True),
        )

    def a_half(m, d, w):
        return remote(
            s1buf.at[m, coord(side // 2, True), half_of(w)], rhalf.at[m, w],
            send_sem.at[0], ar_recv.at[m, w], along(2 * d, True),
        )

    def a_direct(m, d, w):
        return remote(
            s1buf.at[m, coord(d, True)], r1buf.at[m, w, 1],
            send_sem.at[0], ad_recv.at[m], along(d, True),
        )

    def a_agg(m, d, w):
        return remote(
            aggbuf.at[m, w], r1buf.at[m, w, 2],
            send_sem.at[0], ad_recv.at[m], along(2 * d, True),
        )

    def stage_b(m, d, swap):
        send, recv = (send_sem.at[0], c_recv) if swap else (send_sem.at[2], b_recv)
        return remote(
            s2buf.at[coord(d, False), m], (r2sib if swap else r2buf).at[d, m],
            send, recv, along(d, False, swap),
        )

    order = (2, 0, 1)
    for m in order:
        await_bytes(exbuf.at[m], ex_recv.at[m])
        s1buf[m] = (gbuf[core, m].astype(F32) + exbuf[m].astype(F32)).astype(BF16)
        for stage in (a_half, a_relay):
            for d, w in ways:
                stage(m, d, w).start()
    for m in order:
        for d, w in ways:
            a_direct(m, d, w).start()

    for m in order:
        for d, w in ways:
            await_bytes(rhalf.at[:, 0], ar_recv.at[m, w])
            total = s1buf[m, coord(2 * d, True)].astype(F32) + r1buf[m, w, 0].astype(F32)
            aggbuf[m, w] = total.astype(BF16)
            part = half_of(w)
            total = s1buf[m, coord(2 * d, True), part].astype(F32)
            total = total + r1buf[m, w, 0, part].astype(F32) + rhalf[m, w].astype(F32)
            aggbuf[m, w, part] = total.astype(BF16)
            a_agg(m, d, w).start()
    for m in order:
        total = s1buf[m, a1].astype(F32)
        await_bytes(r1buf.at[m, :, pl.ds(1, 2)], ad_recv.at[m])
        for kind in (1, 2):
            for w in range(2):
                total = total + r1buf[m, w, kind].astype(F32)
        s2buf[:, m] = total.astype(BF16)

        def b_start(d, m=m):
            stage_b(m, d, False).start()
            stage_b(m, d, True).start()

        each(b_start)
        stage_b(m, 0, True).start()
    await_bytes(r2buf.at[pl.ds(1, side - 1)], b_recv)
    await_bytes(r2sib, c_recv)
    mine = s2buf[a2].astype(F32)
    other = r2sib[0].astype(F32)
    for d in range(1, side):
        mine = mine + r2buf[d].astype(F32)
        other = other + r2sib[d].astype(F32)
    mom_copy.wait_recv()
    pair = max(1, 16 // rows)
    base_row = pl.multiple_of(lax.div(chip, pair) * (pair * rows), pair * rows)
    for m in range(3):
        lanes = []
        for h in range(2):
            use = jnp.where(core == h, mine[m], other[m])
            lanes += [use[b * rows:(b + 1) * rows] for b in range(blocks)]
        moment = jnp.concatenate(lanes, axis=1) + (mompad[m] + sibmom[m])
        for r in range(own_rows):
            mombuf[0, m, r:r + 1, :] = jnp.where(
                core == 0, moment[r:r + 1], moment[own_rows + r:own_rows + r + 1]
            )
        wide = fast_ref[0, m, pl.ds(base_row, pair * rows), :].astype(F32)
        base = wide[:rows]
        for p in range(1, pair):
            base = jnp.where(lax.rem(chip, pair) == p, wide[p * rows:(p + 1) * rows], base)
        updated = base - moment
        base_rms = jnp.sqrt(jnp.mean(base * base, axis=-1, keepdims=True) + NORM_EPS)
        new_rms = jnp.sqrt(jnp.mean(updated * updated, axis=-1, keepdims=True) + NORM_EPS)
        fresh = updated * (base_rms / new_rms)
        fresh = jnp.where(core == 0, fresh[:, :half], fresh[:, half:])
        parts = [fresh[:, b * LANES:(b + 1) * LANES] for b in range(blocks)]
        packed = jnp.concatenate(parts, axis=0) if blocks > 1 else parts[0]
        rbuf[core, a1, PLACE[0], m] = packed.astype(BF16)

    def g_first(d):
        return remote(
            rbuf.at[core, a1, PLACE[0]], rbuf.at[core, a1, PLACE[side - d]],
            send_sem.at[2], g1_recv.at[min(min(d, side - d), 3) - 1], along(d, False),
        )

    def g_step(g, kind, d, w):
        low, count = ACROSS[g][w] if kind == 3 else GROUPS[g]
        direct = kind == 2 and g == 2
        origin = a1 if kind < 2 or direct else coord(2 * (side - d), True)
        reach = 3 * d if direct else d if kind in (1, 2) else 2 * d
        slab = rbuf.at[core, origin, pl.ds(low, count)]
        spot = (g * 2 + w, 6 + w, 8 + w, 10)[kind]
        return remote(slab, slab, send_sem.at[1], gr_recv.at[spot], along(reach, True))

    def g_steps(kind):
        return [
            (g, kind, d, w) for g in range(3) for d, w in ways if kind < 3 or ACROSS[g][w]
        ]

    def g_sib(n):
        slab = rbuf.at[core, coord(n, True)]
        return remote(slab, slab, send_sem.at[3], gs_recv, sibling)

    def spread(fn):
        for kind in (0, 1):
            for d, w in ways:
                fn(kind, d, w).start()

    def relay_far(fn):
        for d, w in ways:
            fn(0, d, w).wait_recv()
            fn(3, d, w).start()
            fn(2, d, w).start()

    def hand_near(fn, sib):
        sib(0).start()
        for d, w in ways:
            sib((side - 2 * d) % side).start()
            fn(1, d, w).wait_recv()
            sib(side - d).start()

    def hand_far(fn, sib):
        for d, w in ways:
            fn(2, d, w).wait_recv()
            sib((side - 3 * d) % side).start()
        await_bytes(wbuf.at[0, 0], w2_recv.at[6])
        sib(side // 2).start()

    newmom_copy = pltpu.make_async_copy(mombuf, newmom_ref, out_sem.at[1])
    for d in range(1, side):
        g_first(d).start()
    for g, steps in enumerate(GROUP_STEPS):
        low, count = (0, steps) if g else (1, steps)
        await_bytes(rbuf.at[core, a1, pl.ds(low, count)], g1_recv.at[g])
        for kind in (0, 2, 1) if g == 2 else (0, 1):
            for d, w in ways:
                g_step(g, kind, d, w).start()
    g_sib(0).start()

    newmom_copy.start()
    loads[3].wait()
    chunk = tok // 4
    span = tok + chunk
    scale = 1.0 / math.sqrt(hd)
    q_local = lax.broadcasted_iota(jnp.int32, (chunk, span), 0)
    k_local = lax.broadcasted_iota(jnp.int32, (chunk, span), 1)
    window = (k_local > q_local) & (k_local <= q_local + tok)

    def attend(n):
        for i in range(2):
            kv[2 * (3 - n) + i].wait_recv()
        part = pl.ds(n * chunk, chunk)
        reach = pl.ds(n * chunk, span)
        first_key = jnp.where(seq == 0, tok, 0) - n * chunk
        scores = nt(q_ref[part, :], ext_k[reach, :]) * scale
        scores = jnp.where(window & (k_local >= first_key), scores, NEG_LARGE)
        highest = jnp.max(scores, axis=1, keepdims=True)
        expo = jnp.exp(scores - highest)
        total = jnp.sum(expo, axis=1, keepdims=True)
        att[part, :] = nn(expo.astype(BF16), ext_v[reach, :]) / total

    attend(3)

    for g in range(3):
        for d, w in ways:
            g_step(g, 0, d, w).wait_recv()
            if ACROSS[g][w]:
                g_step(g, 3, d, w).start()
            if g < 2:
                g_step(g, 2, d, w).start()
    for copy in kv[2:]:
        copy.start()
    for d, w in ways:
        g_sib((side - 2 * d) % side).start()
    for d, w in ways:
        await_bytes(rbuf.at[0, 0], gr_recv.at[6 + w])
        g_sib(side - d).start()
    for d, w in ways:
        await_bytes(rbuf.at[0, 0], gr_recv.at[8 + w])
        g_sib((side - 3 * d) % side).start()
    await_bytes(rbuf.at[0, 0], gr_recv.at[10])
    g_sib(side // 2).start()
    def unpack(h):
        def body(py, _):
            for m in range(3):
                pieces = []
                for pz in range(side):
                    line, turn = (py, lax.rem(pz + side - z, side)) if h == 0 else (pz, lax.rem(py + side - y, side))
                    place = sum(jnp.where(turn == t, p, 0) for t, p in PLACE.items())
                    tile = rbuf[h, line, place, m].astype(F32)
                    lanes = [tile[b * rows:(b + 1) * rows] for b in range(blocks)]
                    pieces.append(jnp.concatenate(lanes, axis=1))
                part = pl.ds(pl.multiple_of(py * side * rows, side * rows), side * rows)
                renewed[m, part, h * half:(h + 1) * half] = jnp.concatenate(pieces, axis=0).astype(BF16)
            return 0

        lax.fori_loop(0, side, body, 0)

    for h in range(2):
        @pl.when(core == h)
        def _():
            unpack(h)

    await_bytes(rbuf.at[0], gs_recv)
    for h in range(2):
        @pl.when(core != h)
        def _():
            unpack(h)

    def to_right(i):
        piece = comb.at[head, pl.ds(pl.multiple_of(i * chunk, chunk), chunk)]
        return remote(piece, piece, send_sem.at[4], x_recv.at[0, i], right)

    def to_left(i):
        piece = comb.at[head, pl.ds(pl.multiple_of(i * chunk, chunk), chunk)]
        return remote(piece, piece, send_sem.at[4], x_recv.at[1, i], left)

    def forward(i, way):
        source = lax.rem(head + (heads - 1 if way == 0 else 1), heads)
        piece = comb.at[source, pl.ds(pl.multiple_of(i * chunk, chunk), chunk)]
        return remote(piece, piece, send_sem.at[5], f_recv.at[i], right if way == 0 else left)

    def produce(i):
        part = pl.ds(i * chunk, chunk)
        gate = nt(q_ref[part, :], renewed[0])
        up = nt(q_ref[part, :], renewed[1])
        fast_in = (gate * jax.nn.sigmoid(gate) * up).astype(BF16)
        fast_out = nt(fast_in, renewed[2])
        comb[head, part, :] = (att[part, :] + fast_out).astype(BF16)

    inner = (core == 1) | ((z > 0) & (z < side - 1))

    def start_w(early):
        @pl.when(inner if early else jnp.logical_not(inner))
        def _():
            await_bytes(wbuf.at[0, 0, pl.ds(0, side - 1)], w1_recv)
            spread(w_second)

    for n in (3, 2, 1, 0):
        if n < 3:
            attend(n)
        produce(n)
        if n == 3:
            to_right(3).start()
            to_left(3).start()
            start_w(True)
        elif n == 2:
            to_left(2).start()
        elif n == 1:
            to_right(1).start()
            to_right(2).start()
            start_w(False)
        else:
            to_left(0).start()
            to_left(1).start()
            to_right(0).start()

    def pass_on(n):
        if n % 2:
            to_right(n).wait_recv()
            forward(n, 0).start()
        else:
            to_left(n).wait_recv()
            forward(n, 1).start()

    pass_on(3)
    relay_far(w_second)
    pass_on(2)
    hand_near(w_second, w_sib)
    pass_on(1)
    hand_far(w_second, w_sib)
    pass_on(0)
    await_bytes(wbuf.at[0], ws_recv)
    w_rows = wbuf.shape[3]

    def natural(py, _):
        for pz in range(side):
            start = pl.multiple_of((py * side + pz) * 2 * w_rows, 2 * w_rows)
            wnat[pl.ds(start, w_rows), :] = wbuf[0, py, pz]
            wnat[pl.ds(start + w_rows, w_rows), :] = wbuf[1, pz, py]
        return 0

    lax.fori_loop(0, side, natural, 0)

    def out_copy(i):
        part = pl.ds(pl.multiple_of(i * chunk, chunk), chunk)
        return pltpu.make_async_copy(outbuf.at[part], out_ref.at[part], out_sem.at[0])

    def project(source, i, first=False, last=False):
        part = pl.ds(pl.multiple_of(i * chunk, chunk), chunk)
        slab = wnat[pl.ds(pl.multiple_of(source * hd, hd), hd), :]
        value = nn(comb[source, part, :], slab)
        if not first:
            value = acc[part, :] + value
        if last:
            outbuf[part, :] = value.astype(BF16)
            out_copy(i).start()
        else:
            acc[part, :] = value

    lax.fori_loop(0, 4, lambda i, _: (project(head, i, first=True), 0)[1], 0)

    from_left = lax.rem(head + heads - 1, heads)
    from_right = lax.rem(head + 1, heads)
    opposite = lax.rem(head + 2, heads)

    for n in (3, 2, 1, 0):
        (to_left if n % 2 else to_right)(n).wait_recv()
        project(from_left, n)
        project(from_right, n)
    for n in (3, 2, 1, 0):
        forward(n, 1 - n % 2).wait_recv()
        project(opposite, n, last=True)
    newmom_copy.wait()
    pltpu.make_async_copy(outbuf, out_ref, out_sem.at[0]).wait()
    slab = side * tall * LANES
    size = {
        0: 3 * (half * hd) + 3 * 7 * slab + side * 3 * tall * LANES + 2 * 3 * rows * hd,
        1: 2 * tok * hd + 7 * 3 * slab,
        3: 3 * side * slab + (side - 1) * w_rows * hd + 7 * side * w_rows * hd,
        4: side * side * w_rows * hd + 2 * tok * hd,
        5: tok * hd,
    }
    for n, count in size.items():
        part = wnat.at[pl.ds(0, count // hd)]
        remote(part, part, send_sem.at[n], mom_recv, sibling).wait_send()
    part = rbuf.at[0, pl.ds(0, 2), pl.ds(0, side - 1)]
    remote(part, part, send_sem.at[2], mom_recv, sibling).wait_send()


def shards(side, queries, keys, values, rates, fast, momentum, out_proj):
    tok, hd = queries.shape
    heads = lax.axis_size("head")
    ranks = lax.axis_size("seq")
    half = hd // 2
    blocks = half // LANES
    rows = hd // (side * side)
    tall = rows * blocks
    w_rows = out_proj.shape[0]
    grad_scale = 1.0 / math.sqrt(tok * ranks)
    dma = pltpu.SemaphoreType.DMA
    peers = side - 1
    anywhere = pl.BlockSpec(memory_space=pl.ANY)
    return tuple(pl.pallas_call(
        functools.partial(layer_kernel, side, heads, grad_scale),
        out_shape=(
            pltpu.VMEM((tok, hd), BF16),
            pltpu.VMEM(momentum.shape, F32),
        ),
        in_specs=[anywhere] * 7,
        out_specs=(anywhere, anywhere),
        scratch_shapes=[
            pltpu.VMEM((1, tok), F32),
            pltpu.VMEM(momentum.shape, F32),
            pltpu.VMEM((tok, hd), BF16),
            pltpu.VMEM((1, 3, hd, hd), BF16),
            pltpu.VMEM((2 * tok, hd), BF16),
            pltpu.VMEM((2 * tok, hd), BF16),
            pltpu.VMEM((hd, tok), BF16),
            pltpu.VMEM((3, hd, hd), F32),
            pltpu.VMEM((2, 3, side, side, tall, LANES), BF16),
            pltpu.VMEM((3, side, side, tall, LANES), BF16),
            pltpu.VMEM((3, side, side, tall, LANES), BF16),
            pltpu.VMEM((3, 2, 3, side, tall, LANES), BF16),
            pltpu.VMEM((3, 2, side // 2, tall, LANES), BF16),
            pltpu.VMEM((3, 2, side, tall, LANES), BF16),
            pltpu.VMEM((side, 3, tall, LANES), BF16),
            pltpu.VMEM((side, 3, tall, LANES), BF16),
            pltpu.VMEM((side, 3, tall, LANES), BF16),
            pltpu.VMEM((3, rows, hd), F32),
            pltpu.VMEM((3, rows, hd), F32),
            pltpu.VMEM((2, side, side, 3, tall, LANES), BF16),
            pltpu.VMEM((3, hd, hd), BF16),
            pltpu.VMEM((2, side, side, w_rows, hd), BF16),
            pltpu.VMEM((heads * hd, hd), BF16),
            pltpu.VMEM((tok, hd), F32),
            pltpu.VMEM((heads, tok, hd), BF16),
            pltpu.VMEM((tok, hd), F32),
            pltpu.VMEM((tok, hd), BF16),
            pltpu.VMEM(momentum.shape, F32),
            dma((8,)), dma((6,)), dma((3,)), dma((2, 4)), dma(()), dma((3, 2)), dma((3,)), dma(()), dma(()),
            dma((3,)), dma((11,)), dma(()), dma(()), dma((7,)), dma(()), dma((2, 4)), dma((4,)), dma((2,)),
        ],
        compiler_params=pltpu.CompilerParams(
            collective_id=0, has_side_effects=True, vmem_limit_bytes=56 * 1024 * 1024,
        ),
    )(queries, keys, values, rates.reshape(1, tok), fast, momentum, out_proj))


def solution(mesh):
    side = math.isqrt(mesh.shape["seq"] // 2)
    return jax.shard_map(
        functools.partial(shards, side),
        mesh=mesh,
        in_specs=(
            P("seq", "head"),
            P("seq", "head"),
            P("seq", "head"),
            P("seq", "head"),
            P("head", None, None, None),
            P("head", None, "seq", None),
            P("seq", "head"),
        ),
        out_specs=(P("seq", "head"), P("head", None, "seq", None)),
        check_vma=False,
    )
```

```python
import functools
import math

import jax
import jax.numpy as jnp
from jax import lax
from jax.experimental import pallas as pl
from jax.experimental.pallas import tpu as pltpu
from jax.sharding import PartitionSpec as P

MOMENTUM_DECAY = 0.9
NORM_EPS = 1e-06
NEG_LARGE = -1e30
LANES = 128
MESH = pl.DeviceIdType.MESH
PLACE = {7: 0, 0: 1, 1: 2, 2: 3, 6: 4, 3: 5, 4: 6, 5: 7}
GROUPS = ((0, 3), (3, 2), (5, 3))
GROUP_STEPS = (2, 2, 3)
ACROSS = (((0, 3), None), ((3, 1), (4, 1)), (None, (5, 3)))
F32 = jnp.float32
BF16 = jnp.bfloat16


def nt(left, right):
    return lax.dot_general(left, right, (((1,), (1,)), ((), ())), preferred_element_type=F32)


def nn(left, right):
    return lax.dot_general(left, right, (((1,), (0,)), ((), ())), preferred_element_type=F32)


def tn(left, right):
    return lax.dot_general(left, right, (((0,), (0,)), ((), ())), preferred_element_type=F32)


def layer_kernel(
    side, heads, grad_scale,
    q_hbm, k_hbm, v_hbm, rates_hbm, fast_hbm, mom_hbm, proj_hbm,
    out_ref, newmom_ref,
    rates_ref, mom_ref, q_ref, fast_ref, ext_k, ext_v, err_t, grads, gbuf, exbuf, s1buf, r1buf, rhalf, aggbuf, s2buf, r2buf,
    r2sib, mompad, sibmom, rbuf, renewed, wbuf, wnat, att, comb, acc, outbuf, mombuf,
    load_sem, send_sem, ex_recv, kv_recv, mom_recv, ar_recv, ad_recv, b_recv, c_recv,
    g1_recv, gr_recv, gs_recv, w1_recv, w2_recv, ws_recv, x_recv, f_recv, out_sem,
):
    tok = q_ref.shape[0]
    hd = q_ref.shape[1]
    half = hd // 2
    blocks = half // LANES
    chips = side * side
    rows = hd // chips
    own_rows = rows // 2
    tall = rows * blocks

    seq = lax.axis_index("seq")
    head = lax.axis_index("head")
    core = lax.rem(seq, 2)
    chip = lax.div(seq, 2)
    y = lax.div(chip, side)
    z = lax.rem(chip, side)
    a1 = y + core * (z - y)
    a2 = z + core * (y - z)
    ranks = 2 * chips

    def along(d, first, swap=False):
        use_y = (1 - core) if first else core
        py = lax.rem(y + d * use_y, side)
        pz = lax.rem(z + d * (1 - use_y), side)
        return ((py * side + pz) * 2 + (1 - core if swap else core), head)

    sibling = (chip * 2 + 1 - core, head)
    after = (lax.rem(seq + 1, ranks), head)
    right = (seq, lax.rem(head + 1, heads))
    left = (seq, lax.rem(head + heads - 1, heads))
    far = (lax.rem(seq + 2 * core - 1 + ranks, ranks), head)

    def remote(src, dst, send, recv, device):
        return pltpu.make_async_remote_copy(
            src_ref=src, dst_ref=dst, send_sem=send, recv_sem=recv,
            device_id=device, device_id_type=MESH,
        )

    loads = [
        pltpu.make_async_copy(k_hbm, ext_k.at[pl.ds(tok, tok)], load_sem.at[0]),
        pltpu.make_async_copy(fast_hbm.at[:, pl.ds(0, 2)], fast_ref.at[:, pl.ds(0, 2)], load_sem.at[1]),
        pltpu.make_async_copy(v_hbm, ext_v.at[pl.ds(tok, tok)], load_sem.at[2]),
        pltpu.make_async_copy(q_hbm, q_ref, load_sem.at[3]),
        pltpu.make_async_copy(proj_hbm, wbuf.at[core, a1, a2], load_sem.at[4]),
        pltpu.make_async_copy(mom_hbm, mom_ref, load_sem.at[5]),
        pltpu.make_async_copy(rates_hbm, rates_ref, load_sem.at[6]),
        pltpu.make_async_copy(fast_hbm.at[:, pl.ds(2, 1)], fast_ref.at[:, pl.ds(2, 1)], load_sem.at[7]),
    ]
    for n in (0, 1, 6, 2, 7, 5, 4, 3):
        loads[n].start()

    def await_bytes(ref, sem):
        remote(ref, ref, send_sem.at[0], sem, sibling).wait_recv()

    barrier = pltpu.get_barrier_semaphore()

    def greet(d, _):
        for first in (True, False):
            for swap in (True, False):
                device = along(d, first, swap)
                pl.semaphore_signal(barrier, inc=1, device_id=device, device_id_type=MESH)
        return 0

    lax.fori_loop(1, side, greet, 0)
    for device in (sibling, right, left, far):
        pl.semaphore_signal(barrier, inc=1, device_id=device, device_id_type=MESH)

    for n in (0, 1, 6, 2, 7):
        loads[n].wait()

    def gradient(i, first):
        part = pl.ds(pl.multiple_of(i * half, half), half)
        keys = ext_k[tok:, :]
        gate = nt(fast_ref[0, 0, part, :], keys)
        up = nt(fast_ref[0, 1, part, :], keys)
        if first:
            rate_row = -grad_scale * rates_ref[...]
            err_t[...] = (rate_row * ext_v[tok:, :].astype(F32).T).astype(BF16)
        sigma = jax.nn.sigmoid(gate)
        gated = (gate * sigma * up).astype(BF16)
        back = tn(fast_ref[0, 2, :, part], err_t[...])
        grads[2, :, part] = nt(err_t[...], gated)
        d_gate = (back * up * sigma * (1.0 + gate * (1.0 - sigma))).astype(BF16)
        d_up = (back * gate * sigma).astype(BF16)
        grads[0, part, :] = nn(d_gate, keys)
        grads[1, part, :] = nn(d_up, keys)

    def pieces_of(m, py, h):
        line = grads[m, pl.ds(pl.multiple_of(py * side * rows, side * rows), side * rows), h * half:(h + 1) * half]
        line = line.reshape(side, rows, half)
        parts = [line[:, :, b * LANES:(b + 1) * LANES] for b in range(blocks)]
        tile = (jnp.concatenate(parts, axis=1) if blocks > 1 else parts[0]).astype(BF16)
        if h == 0:
            gbuf[0, m, py] = tile
        else:
            gbuf[1, m, :, py] = tile

    def pack_rows(i):
        def body(n, _):
            for m in range(2):
                for h in range(2):
                    pieces_of(m, i * (side // 2) + n, h)
            return 0

        lax.fori_loop(0, side // 2, body, 0)

    def pack_down(i):
        for h in range(2):
            @pl.when(i == h)
            def _():
                lax.fori_loop(0, side, lambda n, _: (pieces_of(2, n, h), 0)[1], 0)

    def ex_down():
        return remote(gbuf.at[1 - core, 2], exbuf.at[2], send_sem.at[0], ex_recv.at[2], sibling)

    def ex_part(m, p, c):
        where = (1 - c, m, pl.ds(p * (side // 2), side // 2))
        if c == 0:
            where = (1 - c, m, slice(None), pl.ds(p * (side // 2), side // 2))
        return remote(
            gbuf.at[where], exbuf.at[where[1:]], send_sem.at[0], ex_recv.at[m], sibling
        )

    def ex_parts(mine):
        for c in range(2):
            p = c if mine else 1 - c

            @pl.when(core == c)
            def _():
                for m in range(2):
                    ex_part(m, p, c).start()

    def each(fn):
        lax.fori_loop(1, side, lambda d, _: (fn(d), 0)[1], 0)

    def w_first(d):
        spot = wbuf.at[core, a1, a2]
        return remote(spot, spot, send_sem.at[3], w1_recv, along(d, False))

    ways = ((side - 1, 0), (1, 1))

    def half_of(w):
        return pl.ds(w * (side // 2), side // 2)

    def coord(d, first):
        return lax.rem((a1 if first else a2) + d, side)

    def w_second(kind, d, w):
        buf = wbuf
        back = side - d
        if kind == 0:
            slab, reach = buf.at[core, a1], 2 * d
        elif kind == 1:
            slab, reach = buf.at[core, a1], d
        elif kind == 2:
            slab, reach = buf.at[core, coord(2 * back, True)], d
        else:
            slab, reach = buf.at[core, coord(2 * back, True), half_of(w)], 2 * d
        spot = (w, 2 + w, 4 + w, 6)[kind]
        return remote(slab, slab, send_sem.at[3], w2_recv.at[spot], along(reach, True))

    def w_sib(n):
        slab = wbuf.at[core, coord(n, True)]
        return remote(slab, slab, send_sem.at[4], ws_recv, sibling)

    gradient(1 - core, True)
    pl.semaphore_wait(barrier, 4 * (side - 1) + 4)
    kv_rows = tok // 4
    kv = [
        remote(
            ext.at[pl.ds(tok + n * kv_rows, kv_rows)], ext.at[pl.ds(n * kv_rows, kv_rows)],
            send_sem.at[1], kv_recv.at[i, n], after,
        )
        for n in (3, 2, 1, 0) for i, ext in enumerate((ext_k, ext_v))
    ]
    for copy in kv[:2]:
        copy.start()
    loads[4].wait()
    each(lambda d: w_first(d).start())
    pack_down(1 - core)
    pack_rows(1 - core)
    ex_down().start()
    ex_parts(False)
    gradient(core, False)

    pack_rows(core)
    ex_parts(True)
    pack_down(core)
    def a_relay(m, d, w):
        return remote(
            s1buf.at[m, coord(3 * d, True)], r1buf.at[m, w, 0],
            send_sem.at[0], ar_recv.at[m, w], along(d, True),
        )

    def a_half(m, d, w):
        return remote(
            s1buf.at[m, coord(side // 2, True), half_of(w)], rhalf.at[m, w],
            send_sem.at[0], ar_recv.at[m, w], along(2 * d, True),
        )

    def a_direct(m, d, w):
        return remote(
            s1buf.at[m, coord(d, True)], r1buf.at[m, w, 1],
            send_sem.at[0], ad_recv.at[m], along(d, True),
        )

    def a_agg(m, d, w):
        return remote(
            aggbuf.at[m, w], r1buf.at[m, w, 2],
            send_sem.at[0], ad_recv.at[m], along(2 * d, True),
        )

    def stage_b(m, d, swap):
        send, recv = (send_sem.at[0], c_recv) if swap else (send_sem.at[2], b_recv)
        return remote(
            s2buf.at[coord(d, False), m], (r2sib if swap else r2buf).at[d, m],
            send, recv, along(d, False, swap),
        )

    order = (2, 0, 1)
    for m in order:
        await_bytes(exbuf.at[m], ex_recv.at[m])
        s1buf[m] = (gbuf[core, m].astype(F32) + exbuf[m].astype(F32)).astype(BF16)
        for stage in (a_half, a_relay):
            for d, w in ways:
                stage(m, d, w).start()
    for m in order:
        for d, w in ways:
            a_direct(m, d, w).start()

    loads[5].wait()
    row_of = lax.broadcasted_iota(jnp.int32, (rows, hd), 0)
    for m in range(3):
        padded = jnp.zeros((rows, hd), F32)
        for r in range(own_rows):
            value = MOMENTUM_DECAY * mom_ref[0, m, r:r + 1, :]
            padded = jnp.where(row_of == r + own_rows * core, jnp.broadcast_to(value, (rows, hd)), padded)
        mompad[m] = padded

    mom_copy = remote(mompad, sibmom, send_sem.at[0], mom_recv, sibling)
    mom_copy.start()

    for m in order:
        for d, w in ways:
            await_bytes(rhalf.at[:, 0], ar_recv.at[m, w])
            total = s1buf[m, coord(2 * d, True)].astype(F32) + r1buf[m, w, 0].astype(F32)
            aggbuf[m, w] = total.astype(BF16)
            part = half_of(w)
            total = s1buf[m, coord(2 * d, True), part].astype(F32)
            total = total + r1buf[m, w, 0, part].astype(F32) + rhalf[m, w].astype(F32)
            aggbuf[m, w, part] = total.astype(BF16)
            a_agg(m, d, w).start()
    for m in order:
        total = s1buf[m, a1].astype(F32)
        await_bytes(r1buf.at[m, :, pl.ds(1, 2)], ad_recv.at[m])
        for kind in (1, 2):
            for w in range(2):
                total = total + r1buf[m, w, kind].astype(F32)
        s2buf[:, m] = total.astype(BF16)

        def b_start(d, m=m):
            stage_b(m, d, False).start()
            stage_b(m, d, True).start()

        each(b_start)
        stage_b(m, 0, True).start()
    await_bytes(r2buf.at[pl.ds(1, side - 1)], b_recv)
    await_bytes(r2sib, c_recv)
    mine = s2buf[a2].astype(F32)
    other = r2sib[0].astype(F32)
    for d in range(1, side):
        mine = mine + r2buf[d].astype(F32)
        other = other + r2sib[d].astype(F32)
    mom_copy.wait_recv()
    pair = max(1, 16 // rows)
    base_row = pl.multiple_of(lax.div(chip, pair) * (pair * rows), pair * rows)
    for m in range(3):
        lanes = []
        for h in range(2):
            use = jnp.where(core == h, mine[m], other[m])
            lanes += [use[b * rows:(b + 1) * rows] for b in range(blocks)]
        moment = jnp.concatenate(lanes, axis=1) + (mompad[m] + sibmom[m])
        for r in range(own_rows):
            mombuf[0, m, r:r + 1, :] = jnp.where(
                core == 0, moment[r:r + 1], moment[own_rows + r:own_rows + r + 1]
            )
        wide = fast_ref[0, m, pl.ds(base_row, pair * rows), :].astype(F32)
        base = wide[:rows]
        for p in range(1, pair):
            base = jnp.where(lax.rem(chip, pair) == p, wide[p * rows:(p + 1) * rows], base)
        updated = base - moment
        base_rms = jnp.sqrt(jnp.mean(base * base, axis=-1, keepdims=True) + NORM_EPS)
        new_rms = jnp.sqrt(jnp.mean(updated * updated, axis=-1, keepdims=True) + NORM_EPS)
        fresh = updated * (base_rms / new_rms)
        fresh = jnp.where(core == 0, fresh[:, :half], fresh[:, half:])
        parts = [fresh[:, b * LANES:(b + 1) * LANES] for b in range(blocks)]
        packed = jnp.concatenate(parts, axis=0) if blocks > 1 else parts[0]
        rbuf[core, a1, PLACE[0], m] = packed.astype(BF16)

    def g_first(d):
        return remote(
            rbuf.at[core, a1, PLACE[0]], rbuf.at[core, a1, PLACE[side - d]],
            send_sem.at[2], g1_recv.at[min(min(d, side - d), 3) - 1], along(d, False),
        )

    def g_step(g, kind, d, w):
        low, count = ACROSS[g][w] if kind == 3 else GROUPS[g]
        direct = kind == 2 and g == 2
        origin = a1 if kind < 2 or direct else coord(2 * (side - d), True)
        reach = 3 * d if direct else d if kind in (1, 2) else 2 * d
        slab = rbuf.at[core, origin, pl.ds(low, count)]
        spot = (g * 2 + w, 6 + w, 8 + w, 10)[kind]
        return remote(slab, slab, send_sem.at[1], gr_recv.at[spot], along(reach, True))

    def g_steps(kind):
        return [
            (g, kind, d, w) for g in range(3) for d, w in ways if kind < 3 or ACROSS[g][w]
        ]

    def g_sib(n):
        slab = rbuf.at[core, coord(n, True)]
        return remote(slab, slab, send_sem.at[3], gs_recv, sibling)

    def spread(fn):
        for kind in (0, 1):
            for d, w in ways:
                fn(kind, d, w).start()

    def relay_far(fn):
        for d, w in ways:
            fn(0, d, w).wait_recv()
            fn(3, d, w).start()
            fn(2, d, w).start()

    def hand_near(fn, sib):
        sib(0).start()
        for d, w in ways:
            sib((side - 2 * d) % side).start()
            fn(1, d, w).wait_recv()
            sib(side - d).start()

    def hand_far(fn, sib):
        for d, w in ways:
            fn(2, d, w).wait_recv()
            sib((side - 3 * d) % side).start()
        await_bytes(wbuf.at[0, 0], w2_recv.at[6])
        sib(side // 2).start()

    newmom_copy = pltpu.make_async_copy(mombuf, newmom_ref, out_sem.at[1])
    for d in range(1, side):
        g_first(d).start()
    for g, steps in enumerate(GROUP_STEPS):
        low, count = (0, steps) if g else (1, steps)
        await_bytes(rbuf.at[core, a1, pl.ds(low, count)], g1_recv.at[g])
        for kind in (0, 2, 1) if g == 2 else (0, 1):
            for d, w in ways:
                g_step(g, kind, d, w).start()
    g_sib(0).start()

    newmom_copy.start()
    loads[3].wait()
    chunk = tok // 4
    span = tok + chunk
    scale = 1.0 / math.sqrt(hd)
    q_local = lax.broadcasted_iota(jnp.int32, (chunk, span), 0)
    k_local = lax.broadcasted_iota(jnp.int32, (chunk, span), 1)
    window = (k_local > q_local) & (k_local <= q_local + tok)

    def attend(n):
        for i in range(2):
            kv[2 * (3 - n) + i].wait_recv()
        part = pl.ds(n * chunk, chunk)
        reach = pl.ds(n * chunk, span)
        first_key = jnp.where(seq == 0, tok, 0) - n * chunk
        scores = nt(q_ref[part, :], ext_k[reach, :]) * scale
        scores = jnp.where(window & (k_local >= first_key), scores, NEG_LARGE)
        highest = jnp.max(scores, axis=1, keepdims=True)
        expo = jnp.exp(scores - highest)
        total = jnp.sum(expo, axis=1, keepdims=True)
        att[part, :] = nn(expo.astype(BF16), ext_v[reach, :]) / total

    attend(3)

    for g in range(3):
        for d, w in ways:
            g_step(g, 0, d, w).wait_recv()
            if ACROSS[g][w]:
                g_step(g, 3, d, w).start()
            if g < 2:
                g_step(g, 2, d, w).start()
    for copy in kv[2:]:
        copy.start()
    for d, w in ways:
        g_sib((side - 2 * d) % side).start()
    for d, w in ways:
        await_bytes(rbuf.at[0, 0], gr_recv.at[6 + w])
        g_sib(side - d).start()
    for d, w in ways:
        await_bytes(rbuf.at[0, 0], gr_recv.at[8 + w])
        g_sib((side - 3 * d) % side).start()
    await_bytes(rbuf.at[0, 0], gr_recv.at[10])
    g_sib(side // 2).start()
    def place_of(turn):
        return sum(jnp.where(turn == t, p, 0) for t, p in PLACE.items())

    def unpack(h):
        fixed = [place_of(lax.rem(pz + side - z, side)) for pz in range(side)] if h == 0 else None

        def body(py, _):
            moving = place_of(lax.rem(py + side - y, side)) if h else None
            for m in range(3):
                pieces = []
                for pz in range(side):
                    line, place = (py, fixed[pz]) if h == 0 else (pz, moving)
                    tile = rbuf[h, line, place, m].astype(F32)
                    lanes = [tile[b * rows:(b + 1) * rows] for b in range(blocks)]
                    pieces.append(jnp.concatenate(lanes, axis=1))
                part = pl.ds(pl.multiple_of(py * side * rows, side * rows), side * rows)
                renewed[m, part, h * half:(h + 1) * half] = jnp.concatenate(pieces, axis=0).astype(BF16)
            return 0

        lax.fori_loop(0, side, body, 0)

    for h in range(2):
        @pl.when(core == h)
        def _():
            unpack(h)

    await_bytes(rbuf.at[0], gs_recv)
    for h in range(2):
        @pl.when(core != h)
        def _():
            unpack(h)

    def to_right(i):
        piece = comb.at[head, pl.ds(pl.multiple_of(i * chunk, chunk), chunk)]
        return remote(piece, piece, send_sem.at[4], x_recv.at[0, i], right)

    def to_left(i):
        piece = comb.at[head, pl.ds(pl.multiple_of(i * chunk, chunk), chunk)]
        return remote(piece, piece, send_sem.at[4], x_recv.at[1, i], left)

    def forward(i, way):
        source = lax.rem(head + (heads - 1 if way == 0 else 1), heads)
        piece = comb.at[source, pl.ds(pl.multiple_of(i * chunk, chunk), chunk)]
        return remote(piece, piece, send_sem.at[5], f_recv.at[i], right if way == 0 else left)

    def produce(i):
        part = pl.ds(i * chunk, chunk)
        gate = nt(q_ref[part, :], renewed[0])
        up = nt(q_ref[part, :], renewed[1])
        fast_in = (gate * jax.nn.sigmoid(gate) * up).astype(BF16)
        fast_out = nt(fast_in, renewed[2])
        comb[head, part, :] = (att[part, :] + fast_out).astype(BF16)

    inner = (core == 1) | ((z > 0) & (z < side - 1))

    def start_w(early):
        @pl.when(inner if early else jnp.logical_not(inner))
        def _():
            await_bytes(wbuf.at[0, 0, pl.ds(0, side - 1)], w1_recv)
            spread(w_second)

    for n in (3, 2, 1, 0):
        if n < 3:
            attend(n)
        produce(n)
        if n == 3:
            to_right(3).start()
            to_left(3).start()
            start_w(True)
        elif n == 2:
            to_left(2).start()
        elif n == 1:
            to_right(1).start()
            to_right(2).start()
            start_w(False)
        else:
            to_left(0).start()
            to_left(1).start()
            to_right(0).start()

    def pass_on(n):
        if n % 2:
            to_right(n).wait_recv()
            forward(n, 0).start()
        else:
            to_left(n).wait_recv()
            forward(n, 1).start()

    pass_on(3)
    relay_far(w_second)
    pass_on(2)
    hand_near(w_second, w_sib)
    pass_on(1)
    hand_far(w_second, w_sib)
    pass_on(0)
    await_bytes(wbuf.at[0], ws_recv)
    w_rows = wbuf.shape[3]

    def natural(py, _):
        for pz in range(side):
            start = pl.multiple_of((py * side + pz) * 2 * w_rows, 2 * w_rows)
            wnat[pl.ds(start, w_rows), :] = wbuf[0, py, pz]
            wnat[pl.ds(start + w_rows, w_rows), :] = wbuf[1, pz, py]
        return 0

    lax.fori_loop(0, side, natural, 0)

    def out_copy(i):
        part = pl.ds(pl.multiple_of(i * chunk, chunk), chunk)
        return pltpu.make_async_copy(outbuf.at[part], out_ref.at[part], out_sem.at[0])

    def project(source, i, first=False, last=False):
        part = pl.ds(pl.multiple_of(i * chunk, chunk), chunk)
        slab = wnat[pl.ds(pl.multiple_of(source * hd, hd), hd), :]
        value = nn(comb[source, part, :], slab)
        if not first:
            value = acc[part, :] + value
        if last:
            outbuf[part, :] = value.astype(BF16)
            out_copy(i).start()
        else:
            acc[part, :] = value

    lax.fori_loop(0, 4, lambda i, _: (project(head, i, first=True), 0)[1], 0)

    from_left = lax.rem(head + heads - 1, heads)
    from_right = lax.rem(head + 1, heads)
    opposite = lax.rem(head + 2, heads)

    for n in (3, 2, 1, 0):
        (to_left if n % 2 else to_right)(n).wait_recv()
        project(from_left, n)
        project(from_right, n)
    for n in (3, 2, 1, 0):
        forward(n, 1 - n % 2).wait_recv()
        project(opposite, n, last=True)
    newmom_copy.wait()
    pltpu.make_async_copy(outbuf, out_ref, out_sem.at[0]).wait()
    slab = side * tall * LANES
    size = {
        0: 3 * (half * hd) + 3 * 7 * slab + side * 3 * tall * LANES + 2 * 3 * rows * hd,
        1: 2 * tok * hd + 7 * 3 * slab,
        3: 3 * side * slab + (side - 1) * w_rows * hd + 7 * side * w_rows * hd,
        4: side * side * w_rows * hd + 2 * tok * hd,
        5: tok * hd,
    }
    for n, count in size.items():
        part = wnat.at[pl.ds(0, count // hd)]
        remote(part, part, send_sem.at[n], mom_recv, sibling).wait_send()
    part = rbuf.at[0, pl.ds(0, 2), pl.ds(0, side - 1)]
    remote(part, part, send_sem.at[2], mom_recv, sibling).wait_send()


def shards(side, queries, keys, values, rates, fast, momentum, out_proj):
    tok, hd = queries.shape
    heads = lax.axis_size("head")
    ranks = lax.axis_size("seq")
    half = hd // 2
    blocks = half // LANES
    rows = hd // (side * side)
    tall = rows * blocks
    w_rows = out_proj.shape[0]
    grad_scale = 1.0 / math.sqrt(tok * ranks)
    dma = pltpu.SemaphoreType.DMA
    peers = side - 1
    anywhere = pl.BlockSpec(memory_space=pl.ANY)
    return tuple(pl.pallas_call(
        functools.partial(layer_kernel, side, heads, grad_scale),
        out_shape=(
            pltpu.VMEM((tok, hd), BF16),
            pltpu.VMEM(momentum.shape, F32),
        ),
        in_specs=[anywhere] * 7,
        out_specs=(anywhere, anywhere),
        scratch_shapes=[
            pltpu.VMEM((1, tok), F32),
            pltpu.VMEM(momentum.shape, F32),
            pltpu.VMEM((tok, hd), BF16),
            pltpu.VMEM((1, 3, hd, hd), BF16),
            pltpu.VMEM((2 * tok, hd), BF16),
            pltpu.VMEM((2 * tok, hd), BF16),
            pltpu.VMEM((hd, tok), BF16),
            pltpu.VMEM((3, hd, hd), F32),
            pltpu.VMEM((2, 3, side, side, tall, LANES), BF16),
            pltpu.VMEM((3, side, side, tall, LANES), BF16),
            pltpu.VMEM((3, side, side, tall, LANES), BF16),
            pltpu.VMEM((3, 2, 3, side, tall, LANES), BF16),
            pltpu.VMEM((3, 2, side // 2, tall, LANES), BF16),
            pltpu.VMEM((3, 2, side, tall, LANES), BF16),
            pltpu.VMEM((side, 3, tall, LANES), BF16),
            pltpu.VMEM((side, 3, tall, LANES), BF16),
            pltpu.VMEM((side, 3, tall, LANES), BF16),
            pltpu.VMEM((3, rows, hd), F32),
            pltpu.VMEM((3, rows, hd), F32),
            pltpu.VMEM((2, side, side, 3, tall, LANES), BF16),
            pltpu.VMEM((3, hd, hd), BF16),
            pltpu.VMEM((2, side, side, w_rows, hd), BF16),
            pltpu.VMEM((heads * hd, hd), BF16),
            pltpu.VMEM((tok, hd), F32),
            pltpu.VMEM((heads, tok, hd), BF16),
            pltpu.VMEM((tok, hd), F32),
            pltpu.VMEM((tok, hd), BF16),
            pltpu.VMEM(momentum.shape, F32),
            dma((8,)), dma((6,)), dma((3,)), dma((2, 4)), dma(()), dma((3, 2)), dma((3,)), dma(()), dma(()),
            dma((3,)), dma((11,)), dma(()), dma(()), dma((7,)), dma(()), dma((2, 4)), dma((4,)), dma((2,)),
        ],
        compiler_params=pltpu.CompilerParams(
            collective_id=0, has_side_effects=True, vmem_limit_bytes=56 * 1024 * 1024,
        ),
    )(queries, keys, values, rates.reshape(1, tok), fast, momentum, out_proj))


def solution(mesh):
    side = math.isqrt(mesh.shape["seq"] // 2)
    return jax.shard_map(
        functools.partial(shards, side),
        mesh=mesh,
        in_specs=(
            P("seq", "head"),
            P("seq", "head"),
            P("seq", "head"),
            P("seq", "head"),
            P("head", None, None, None),
            P("head", None, "seq", None),
            P("seq", "head"),
        ),
        out_specs=(P("seq", "head"), P("head", None, "seq", None)),
        check_vma=False,
    )
```
